512 devices in a mesh: seq: 32 (over y, x, core), head: 16 (over z).
Axes of the slice: x: 4, y: 4, z: 16, core: 2. Of those that a mesh axis runs over, the one named last changes fastest.
Arguments:
- x_in: bfloat16 [8192, 8192], P('seq', 'head'), may hold values from -6 to 6
- b_in: bfloat16 [8192, 128], P(('seq', 'head')), may hold values from -0.5 to 0.5
- c_in: bfloat16 [8192, 128], P(('seq', 'head')), may hold values from -0.5 to 0.5
- decay_codes: int32 [128, 8192], P('head', 'seq'), may hold values from 0 to 7168
- decay_rate: float32 [128], P('head'), may hold values from 0 to 0.05
- skip_gain: float32 [128], P('head'), may hold values from 0.5 to 1.5
- out_grad: bfloat16 [8192, 8192], P('seq', 'head'), may hold values from -6 to 6
Outputs:
- ssm_out: bfloat16 [8192, 8192], P('seq', 'head')
- input_grad: bfloat16 [8192, 8192], P('seq', 'head')
- grad_b: float32 [8192, 128], P(('seq', 'head'))
- grad_c: float32 [8192, 128], P(('seq', 'head'))
The draws below stay inside these ranges and needn't reach their ends.
All inputs are finite; a program needn't handle non-finite values.
Results may differ from the reference program's by a relative error of at most 0.005.
Values may be sent and summed in bfloat16 or wider, within the bound.
No kernel may reach another device: no remote copies, remote signals or barrier semaphores. Data moves between devices by JAX's collectives and lax.ppermute only.
A program may use at most 64 MiB of HBM per device.

```python
import jax
import jax.numpy as jnp
from jax import lax

HEADS = 128
HEAD_DIM = 64
STATE = 128
BLOCK = 256
TOKENS = 8192


def draw_decay_codes(key, part):
    base_key, place_key, level_key = jax.random.split(jax.random.fold_in(key, 17), 3)
    base = jax.random.randint(base_key, (HEADS, TOKENS), 0, 1024)
    places = jax.random.permutation(place_key, TOKENS)[:3]
    levels = jax.random.randint(level_key, (HEADS, 3), 2, 7)
    matches = (jnp.arange(TOKENS)[:, None] == places[None, :]).astype(jnp.int32)
    raised = jnp.einsum('hs,ts->ht', levels, matches)
    return (base + 1024 * raised).astype(jnp.int32)


def draw_decay_rate(key, part):
    pick_key, value_key = jax.random.split(jax.random.fold_in(key, 23))
    slow_share = 0.7
    picks = jax.random.uniform(pick_key, (HEADS,))
    spread = jax.random.uniform(value_key, (HEADS,))
    slow_rate = jnp.exp(jnp.log(0.2 / TOKENS) + spread * jnp.log(5.0))
    fast_rate = jnp.exp(jnp.log(0.02) + spread * jnp.log(50.0 / 30.0))
    return jnp.where(picks < slow_share, slow_rate, fast_rate).astype(jnp.float32)


def block_scale(own_key, shape, cuts, least, largest):
    level = 1.0
    for dim, shards_of in cuts:
        heights = jax.random.uniform(jax.random.fold_in(jax.random.fold_in(own_key, 6), dim), (shards_of,), jnp.float32, least / len(cuts), largest / len(cuts))
        level = level * jnp.repeat(jnp.exp(heights), shape[dim] // shards_of).reshape((-1,) + (1,) * (len(shape) - 1 - dim))
    return level


def normal_values(key, extent, deviation, limit, cuts=(), kind=jnp.bfloat16):
    array = jax.random.normal(key, extent, jnp.float32) * deviation
    if len(cuts) > 0:
        array = block_scale(key, extent, cuts, -0.22, 0.18) * array
    return jnp.clip(array, min=-limit, max=limit).astype(kind)


def setup_inputs(seed: int = 0) -> dict:
    key_of = jax.random.split(jax.random.key(seed), 8)
    return {
        "x_in": normal_values(key_of[0], (TOKENS, HEADS * HEAD_DIM), 1.0, 6.0, ((0, 32), (1, 16))),
        "b_in": normal_values(key_of[1], (TOKENS, STATE), ((STATE * TOKENS) ** -0.25), 0.5, ((0, 512),)),
        "c_in": normal_values(key_of[2], (TOKENS, STATE), ((STATE * TOKENS) ** -0.25), 0.5, ((0, 512),)),
        "decay_codes": draw_decay_codes(jax.random.fold_in(key_of[7], 71), 0),
        "decay_rate": draw_decay_rate(jax.random.fold_in(key_of[7], 71), 0),
        "skip_gain": jnp.clip(0.5 + 1.0 * jax.random.uniform(key_of[5], (HEADS,), jnp.float32) ** block_scale(key_of[5], (HEADS,), ((0, 16),), -0.2, 0.2), 0.5, 1.5),
        "out_grad": normal_values(key_of[6], (TOKENS, HEADS * HEAD_DIM), 1.0, 6.0, ((0, 32), (1, 16))),
    }


def exact(form, operands):
    return jnp.einsum(form, *operands, precision=lax.Precision.HIGHEST)


def decode(decay_labels, decay_speeds):
    time_delta = 0.5 + (decay_labels % 1024).astype(jnp.float32) / 1024.0
    spike_loss_term = 0.1 * (decay_labels // 1024).astype(jnp.float32)
    return time_delta, -decay_speeds[:, None] * time_delta - spike_loss_term


def summarize(cumul, b_block, c_block, driven, cotangent):
    tail = jnp.exp(cumul[:, -1:] - cumul)
    state_part = exact("hj,jn,jhp->hpn", (tail, b_block.astype(jnp.float32), driven))
    adjoint_part = exact("hi,in,ihp->hpn", (jnp.exp(cumul), c_block.astype(jnp.float32), cotangent))
    return state_part, adjoint_part


def within(cumul, b_block, c_block, driven, cotangent):
    width = cumul.shape[1]
    causal = lax.broadcasted_iota(jnp.int32, (width, width), 0) >= lax.broadcasted_iota(jnp.int32, (width, width), 1)
    spread = cumul[:, :, None] - cumul[:, None, :]
    weights = jnp.where(causal, jnp.exp(jnp.where(causal, spread, 0.0)), 0.0)
    scores = jnp.dot(c_block, b_block.T, preferred_element_type=jnp.float32)
    mixed = (weights * scores).astype(jnp.bfloat16).astype(jnp.float32)
    out_part = exact("hij,jhp->ihp", (mixed, driven))
    drive_grad = exact("hij,ihp->jhp", (mixed, cotangent))
    paired = (weights * exact("ihp,jhp->hij", (cotangent, driven))).astype(jnp.bfloat16).astype(jnp.float32)
    c_grad = exact("hij,jn->in", (paired, b_block.astype(jnp.float32)))
    b_grad = exact("hij,in->jn", (paired, c_block.astype(jnp.float32)))
    return out_part, drive_grad, c_grad, b_grad


def reference(x_in, b_in, c_in, decay_codes, decay_rate, skip_gain, out_grad):
    head_count, token_count = decay_codes.shape
    blocks = token_count // BLOCK
    time_delta, log_decay = decode(decay_codes, decay_rate)
    inputs = x_in.astype(jnp.float32).reshape(blocks, BLOCK, head_count, HEAD_DIM)
    cotangent = out_grad.astype(jnp.float32).reshape(blocks, BLOCK, head_count, HEAD_DIM)
    step_tokens = time_delta.reshape(head_count, blocks, BLOCK).transpose(1, 2, 0)[..., None]
    driven = (inputs * step_tokens).astype(jnp.bfloat16).astype(jnp.float32)
    cumul = jnp.cumsum(log_decay.reshape(head_count, blocks, BLOCK), axis=2).transpose(1, 0, 2)
    input_matrix_blocks = b_in.reshape(blocks, BLOCK, STATE)
    c_blocks = c_in.reshape(blocks, BLOCK, STATE)
    blank_state = jnp.zeros((head_count, HEAD_DIM, STATE), jnp.float32)

    def ahead(running, group):
        cumul_b, b_block, c_block, driven_b, cot_b = group
        state_part, adjoint_part = summarize(cumul_b, b_block, c_block, driven_b, cot_b)
        out_part, drive_grad, c_grad, b_grad = within(cumul_b, b_block, c_block, driven_b, cot_b)
        growth = jnp.exp(cumul_b)
        out_cross = exact("hi,hpn,in->ihp", (growth, running, c_block.astype(jnp.float32)))
        c_cross = exact("hi,ihp,hpn->in", (growth, cot_b, running))
        next_device_state = jnp.exp(cumul_b[:, -1])[:, None, None] * running + state_part
        return next_device_state, (out_part + out_cross, c_grad + c_cross, drive_grad, b_grad, adjoint_part)

    last_state, gathered = lax.scan(ahead, blank_state, (cumul, input_matrix_blocks, c_blocks, driven, cotangent))
    out_sum, c_sum, drive_grad, b_grad, adjoint_parts = gathered

    def behind(running, group):
        cumul_b, b_block, driven_b, adjoint_part = group
        tail = jnp.exp(cumul_b[:, -1:] - cumul_b)
        drive_cross = exact("hj,hpn,jn->jhp", (tail, running, b_block.astype(jnp.float32)))
        b_cross = exact("hj,jhp,hpn->jn", (tail, driven_b, running))
        next_device_state = jnp.exp(cumul_b[:, -1])[:, None, None] * running + adjoint_part
        return next_device_state, (drive_cross, b_cross)

    first_adjoint, crossed = lax.scan(behind, blank_state, (cumul, input_matrix_blocks, driven, adjoint_parts), reverse=True)
    drive_cross, b_cross = crossed
    gain = skip_gain[None, None, :, None]
    ssm_out = (out_sum + gain * inputs).astype(jnp.bfloat16).reshape(token_count, head_count * HEAD_DIM)
    input_grad = (gain * cotangent + step_tokens * (drive_grad + drive_cross)).astype(jnp.bfloat16)
    input_grad = input_grad.reshape(token_count, head_count * HEAD_DIM)
    grad_b = (b_grad + b_cross).reshape(token_count, STATE)
    grad_c = c_sum.reshape(token_count, STATE)
    return ssm_out, input_grad, grad_b, grad_c
```

```python
import functools

import jax
import jax.numpy as jnp
from jax import lax
from jax.experimental import pallas as pl
from jax.experimental.pallas import tpu as pltpu
from jax.sharding import PartitionSpec as P

HEAD_DIM = 64
STATE = 128
BLOCK = 256
BF = jnp.bfloat16
F32 = jnp.float32


def dg(a, b, ca, cb):
    return lax.dot_general(a, b, (((ca,), (cb,)), ((), ())), preferred_element_type=F32)


def pieces(v, count):
    out = []
    for _ in range(count):
        part = v.astype(BF)
        out.append(part)
        v = v - part.astype(F32)
    return out


def split_dot(v, b, ca, cb):
    hi, lo = pieces(v, 2)
    return dg(hi, b, ca, cb) + dg(lo, b, ca, cb)


def spread_rows(rows, count):
    heads = rows.shape[0]
    stacked = jnp.concatenate([p.astype(F32) for p in pieces(rows, count)], axis=0).astype(BF)
    k = heads * count
    row = lax.broadcasted_iota(jnp.int32, (k, heads * HEAD_DIM), 0) % heads
    col = lax.broadcasted_iota(jnp.int32, (k, heads * HEAD_DIM), 1) // HEAD_DIM
    pick = jnp.where(row == col, 1.0, 0.0).astype(BF)
    return dg(stacked, pick, 0, 0)


def decode(codes, rate_ref):
    heads, tokens = codes.shape
    head = lax.broadcasted_iota(jnp.int32, (heads, tokens), 0)
    rate = jnp.zeros((heads, tokens), F32)
    for h in range(heads):
        rate = jnp.where(head == h, rate_ref[h], rate)
    delta = 0.5 + (codes & 1023).astype(F32) / 1024.0
    log_decay = -rate * delta - 0.1 * (codes >> 10).astype(F32)
    return delta, log_decay


def running_sum(log_decay):
    tokens = log_decay.shape[1]
    i = lax.broadcasted_iota(jnp.int32, (tokens, tokens), 0)
    j = lax.broadcasted_iota(jnp.int32, (tokens, tokens), 1)
    upper = jnp.where(i <= j, 1.0, 0.0).astype(BF)
    return sum(dg(p, upper, 1, 0) for p in pieces(log_decay, 3)[::-1])


def common(x_ref, dy_ref, codes_ref, rate_ref):
    delta, log_decay = decode(codes_ref[...], rate_ref)
    cumul = running_sum(log_decay)
    total = cumul[:, BLOCK - 1 :]
    growth = jnp.exp(cumul)
    tail = jnp.exp(total - cumul)
    delta_x = spread_rows(delta, 2)
    growth_x = spread_rows(growth, 3)
    tail_x = spread_rows(tail, 3)
    x = x_ref[...].astype(F32)
    dy = dy_ref[...].astype(F32)
    driven = (x * delta_x).astype(BF)
    return cumul, total, delta_x, growth_x, tail_x, x, dy, driven


def both(bc_ref):
    half = bc_ref.shape[1] // 2
    b = bc_ref[:, :half, :].reshape(BLOCK, STATE)
    c = bc_ref[:, half:, :].reshape(BLOCK, STATE)
    return b, c


def summary_kernel(bc_ref, x_ref, dy_ref, codes_ref, rate_ref, send_ref):
    b, c = both(bc_ref)
    _, total, _, growth_x, tail_x, _, dy, driven = common(x_ref, dy_ref, codes_ref, rate_ref)
    parts = send_ref.shape[0]
    state = split_dot(driven.astype(F32) * tail_x, b, 0, 0)
    adjoint = split_dot(dy * growth_x, c, 0, 0)
    send_ref[:, 0:16, :] = state.astype(BF).reshape(parts, 16, STATE)
    send_ref[:, 16:32, :] = adjoint.astype(BF).reshape(parts, 16, STATE)
    heads = total.shape[0]
    decay = jnp.exp(total)
    hi, mid, low = [p.astype(F32) for p in pieces(decay, 3)]
    row = lax.broadcasted_iota(jnp.int32, (8, STATE), 0)
    per = parts // heads
    for h in range(heads):
        tile = jnp.where(
            row == 0, hi[h : h + 1, :], jnp.where(row == 1, mid[h : h + 1, :], low[h : h + 1, :])
        ).astype(BF)
        for q in range(per):
            send_ref[h * per + q, 32:40, :] = tile


def scan_kernel(got_ref, send_ref):
    count = got_ref.shape[0]
    decays = []
    for k in range(count):
        tile = got_ref[k, 32:40, :].astype(F32)
        decays.append(tile[0:1] + tile[1:2] + tile[2:3])
    run = jnp.zeros((16, STATE), F32)
    for k in range(count):
        send_ref[k, 0:16, :] = run.astype(BF)
        run = decays[k] * run + got_ref[k, 0:16, :].astype(F32)
    run = jnp.zeros((16, STATE), F32)
    for k in reversed(range(count)):
        send_ref[k, 16:32, :] = run.astype(BF)
        run = decays[k] * run + got_ref[k, 16:32, :].astype(F32)


def finish_kernel(
    bc_ref, x_ref, dy_ref, codes_ref, rate_ref, gain_ref, in_ref, out_ref, grad_ref, sums_ref
):
    b, c = both(bc_ref)
    cumul, total, delta_x, growth_x, tail_x, x, dy, driven = common(
        x_ref, dy_ref, codes_ref, rate_ref
    )
    heads = total.shape[0]
    width = heads * HEAD_DIM
    i = lax.broadcasted_iota(jnp.int32, (BLOCK, BLOCK), 0)
    j = lax.broadcasted_iota(jnp.int32, (BLOCK, BLOCK), 1)
    causal = i >= j
    lower = jnp.where(causal, 1.0, 0.0).astype(BF)
    _, log_decay = decode(codes_ref[...], rate_ref)
    cumul_t = sum(dg(lower, p, 1, 1) for p in pieces(log_decay, 3)[::-1])
    scores = dg(c, b, 1, 1)
    low_dy = dy_ref[...]
    lane = lax.broadcasted_iota(jnp.int32, (BLOCK, 2 * HEAD_DIM), 1)
    first = lane < HEAD_DIM
    zero = jnp.zeros((BLOCK, 2 * HEAD_DIM), BF)
    paired = jnp.zeros((BLOCK, BLOCK), F32)
    outs, drives = [], []
    for pair in range(heads // 2):
        cut = slice(pair * 2 * HEAD_DIM, (pair + 1) * 2 * HEAD_DIM)
        u, g = driven[:, cut], low_dy[:, cut]
        made = []
        for side in range(2):
            h = 2 * pair + side
            spread = cumul_t[:, h : h + 1] - cumul[h : h + 1, :]
            weights = jnp.exp(jnp.where(causal, spread, -1e30))
            mixed = (weights * scores).astype(BF)
            own = first if side == 0 else jnp.logical_not(first)
            raw = dg(jnp.where(own, g, zero), u, 1, 1)
            paired = paired + (weights * raw).astype(BF).astype(F32)
            made.append((dg(mixed, u, 1, 0), dg(mixed, g, 0, 0)))
        outs.append(jnp.where(first, made[0][0], made[1][0]))
        drives.append(jnp.where(first, made[0][1], made[1][1]))
    out_part = jnp.concatenate(outs, axis=1)
    drive_grad = jnp.concatenate(drives, axis=1)
    state = in_ref[:, 0:16, :].reshape(width, STATE)
    adjoint = in_ref[:, 16:32, :].reshape(width, STATE)
    chan = lax.broadcasted_iota(jnp.int32, (1, width), 1) // HEAD_DIM
    gain = jnp.zeros((1, width), F32)
    for h in range(heads):
        gain = jnp.where(chan == h, gain_ref[h], gain)
    out_ref[...] = (out_part + growth_x * dg(c, state, 1, 1) + gain * x).astype(BF)
    grad_ref[...] = (
        gain * dy + delta_x * (drive_grad + tail_x * dg(b, adjoint, 1, 1))
    ).astype(BF)
    b_sum = split_dot(paired, c, 0, 0) + split_dot(driven.astype(F32) * tail_x, adjoint, 1, 0)
    c_sum = split_dot(paired, b, 1, 0) + split_dot(dy * growth_x, state, 1, 0)
    shape = sums_ref.shape[:2] + (STATE,)
    sums_ref[:, :, 0:STATE] = b_sum.astype(BF).reshape(shape)
    sums_ref[:, :, STATE:] = c_sum.astype(BF).reshape(shape)


def total_kernel(got_ref, b_ref, c_ref):
    acc = got_ref[0].astype(F32)
    for k in range(1, got_ref.shape[0]):
        acc = acc + got_ref[k].astype(F32)
    b_ref[...] = acc[:, 0:STATE]
    c_ref[...] = acc[:, STATE:]


VMEM = functools.partial(pl.BlockSpec, memory_space=pltpu.VMEM)
SMEM = functools.partial(pl.BlockSpec, memory_space=pltpu.SMEM)


def exchange(x, axis):
    return lax.all_to_all(x, axis, 0, 0, tiled=True)


def local(x_in, b_in, c_in, decay_codes, decay_rate, skip_gain, out_grad):
    seqs, groups = lax.axis_size("seq"), lax.axis_size("head")
    rows = b_in.shape[0]
    mine = jnp.concatenate([b_in, c_in], axis=0)
    bc = exchange(jnp.broadcast_to(mine[None], (groups, 2 * rows, STATE)), "head")
    send = pl.pallas_call(
        summary_kernel,
        out_shape=jax.ShapeDtypeStruct((seqs, 40, STATE), BF),
        in_specs=[VMEM(), VMEM(), VMEM(), VMEM(), SMEM()],
        out_specs=VMEM(),
        name="summary",
    )(bc, x_in, out_grad, decay_codes, decay_rate)
    got = exchange(send, "seq")
    back = pl.pallas_call(
        scan_kernel,
        out_shape=jax.ShapeDtypeStruct((seqs, 32, STATE), BF),
        in_specs=[VMEM()],
        out_specs=VMEM(),
        name="scan",
    )(got)
    carried = exchange(back, "seq")
    ssm_out, input_grad, sums = pl.pallas_call(
        finish_kernel,
        out_shape=(
            jax.ShapeDtypeStruct(x_in.shape, BF),
            jax.ShapeDtypeStruct(x_in.shape, BF),
            jax.ShapeDtypeStruct((groups, rows, 2 * STATE), BF),
        ),
        in_specs=[VMEM(), VMEM(), VMEM(), VMEM(), SMEM(), SMEM(), VMEM()],
        out_specs=(VMEM(), VMEM(), VMEM()),
        name="finish",
    )(bc, x_in, out_grad, decay_codes, decay_rate, skip_gain, carried)
    grad_b, grad_c = pl.pallas_call(
        total_kernel,
        out_shape=(jax.ShapeDtypeStruct((rows, STATE), F32),) * 2,
        in_specs=[VMEM()],
        out_specs=(VMEM(), VMEM()),
        name="total",
    )(exchange(sums, "head"))
    return ssm_out, input_grad, grad_b, grad_c


def solution(mesh):
    placed = (
        P("seq", "head"),
        P(("seq", "head"), None),
        P(("seq", "head"), None),
        P("head", "seq"),
        P("head"),
        P("head"),
        P("seq", "head"),
    )
    return jax.shard_map(
        local,
        mesh=mesh,
        in_specs=placed,
        out_specs=(
            P("seq", "head"),
            P("seq", "head"),
            P(("seq", "head"), None),
            P(("seq", "head"), None),
        ),
        check_vma=False,
    )
```

```python
import jax
import jax.numpy as jnp
from jax import lax
from jax.experimental import pallas as pl
from jax.experimental.pallas import tpu as pltpu
from jax.sharding import PartitionSpec as P

HEAD_DIM = 64
STATE = 128
BLOCK = 256
BF = jnp.bfloat16
F32 = jnp.float32


def dg(a, b, ca, cb):
    return lax.dot_general(a, b, (((ca,), (cb,)), ((), ())), preferred_element_type=F32)


def pieces(v, count):
    out = []
    for _ in range(count):
        part = v.astype(BF)
        out.append(part)
        v = v - part.astype(F32)
    return out


def split_dot(v, b, ca, cb):
    hi, lo = pieces(v, 2)
    return dg(hi, b, ca, cb) + dg(lo, b, ca, cb)


def stack(rows, count):
    return jnp.concatenate([p.astype(F32) for p in pieces(rows, count)], axis=0).astype(BF)


def expand(stacked, heads):
    shape = (stacked.shape[0], heads * HEAD_DIM)
    row = lax.broadcasted_iota(jnp.int32, shape, 0) % heads
    col = lax.broadcasted_iota(jnp.int32, shape, 1) // HEAD_DIM
    pick = jnp.where(row == col, 1.0, 0.0).astype(BF)
    return dg(stacked, pick, 0, 0)


def decode(codes, rate_ref):
    heads, tokens = codes.shape
    head = lax.broadcasted_iota(jnp.int32, (heads, tokens), 0)
    rate = jnp.zeros((heads, tokens), F32)
    for h in range(heads):
        rate = jnp.where(head == h, rate_ref[h], rate)
    delta = 0.5 + (codes & 1023).astype(F32) / 1024.0
    log_decay = -rate * delta - 0.1 * (codes >> 10).astype(F32)
    return delta, log_decay


def running_sum(log_decay):
    tokens = log_decay.shape[1]
    i = lax.broadcasted_iota(jnp.int32, (tokens, tokens), 0)
    j = lax.broadcasted_iota(jnp.int32, (tokens, tokens), 1)
    upper = jnp.where(i <= j, 1.0, 0.0).astype(BF)
    return sum(dg(p, upper, 1, 0) for p in pieces(log_decay, 3)[::-1])


def both(bc_ref):
    half = bc_ref.shape[1] // 2
    b = bc_ref[:, :half, :].reshape(BLOCK, STATE)
    c = bc_ref[:, half:, :].reshape(BLOCK, STATE)
    return b, c


def prepare_kernel(x_ref, dy_ref, codes_ref, rate_ref, td_ref, gd_ref, grow_ref, dt_ref, e_ref):
    delta, log_decay = decode(codes_ref[...], rate_ref)
    cumul = running_sum(log_decay)
    heads = delta.shape[0]
    total = cumul[:, BLOCK - 1 :]
    growth = stack(jnp.exp(cumul), 3)
    tail = jnp.exp(total - cumul)
    driven = (x_ref[...].astype(F32) * expand(stack(delta, 2), heads)).astype(BF)
    td_ref[0], td_ref[1] = pieces(driven.astype(F32) * expand(stack(tail, 3), heads), 2)
    gd_ref[0], gd_ref[1] = pieces(dy_ref[...].astype(F32) * expand(growth, heads), 2)
    grow_ref[...] = growth
    dt_ref[...] = stack(delta * tail, 3)
    hi, mid, low = [p.astype(F32) for p in pieces(jnp.exp(total), 3)]
    row = lax.broadcasted_iota(jnp.int32, (8, STATE), 0)
    for h in range(heads):
        e_ref[h] = jnp.where(
            row == 0, hi[h : h + 1, :], jnp.where(row == 1, mid[h : h + 1, :], low[h : h + 1, :])
        ).astype(BF)


def summary_kernel(bc_ref, td_ref, gd_ref, e_ref, send_ref):
    b, c = both(bc_ref)
    parts, heads = send_ref.shape[0], e_ref.shape[0]
    state = dg(td_ref[0], b, 0, 0) + dg(td_ref[1], b, 0, 0)
    adjoint = dg(gd_ref[0], c, 0, 0) + dg(gd_ref[1], c, 0, 0)
    send_ref[:, 0:16, :] = state.astype(BF).reshape(parts, 16, STATE)
    send_ref[:, 16:32, :] = adjoint.astype(BF).reshape(parts, 16, STATE)
    per = parts // heads
    for h in range(heads):
        for q in range(per):
            send_ref[h * per + q, 32:40, :] = e_ref[h]


def scan_kernel(got_ref, send_ref):
    count = got_ref.shape[0]
    decays = []
    for k in range(count):
        tile = got_ref[k, 32:40, :].astype(F32)
        decays.append(tile[0:1] + tile[1:2] + tile[2:3])
    run = jnp.zeros((16, STATE), F32)
    for k in range(count):
        send_ref[k, 0:16, :] = run.astype(BF)
        run = decays[k] * run + got_ref[k, 0:16, :].astype(F32)
    run = jnp.zeros((16, STATE), F32)
    for k in reversed(range(count)):
        send_ref[k, 16:32, :] = run.astype(BF)
        run = decays[k] * run + got_ref[k, 16:32, :].astype(F32)


def within_kernel(
    bc_ref, x_ref, dy_ref, codes_ref, rate_ref, gain_ref, out_ref, grad_ref, sums_ref
):
    b, c = both(bc_ref)
    delta, log_decay = decode(codes_ref[...], rate_ref)
    cumul = running_sum(log_decay)
    heads = cumul.shape[0]
    delta_x = expand(stack(delta, 2), heads)
    driven = (x_ref[...].astype(F32) * delta_x).astype(BF)
    i = lax.broadcasted_iota(jnp.int32, (BLOCK, BLOCK), 0)
    j = lax.broadcasted_iota(jnp.int32, (BLOCK, BLOCK), 1)
    causal = i >= j
    lower = jnp.where(causal, 1.0, 0.0).astype(BF)
    cumul_t = sum(dg(lower, p, 1, 1) for p in pieces(log_decay, 3)[::-1])
    scores = dg(c, b, 1, 1)
    lane = lax.broadcasted_iota(jnp.int32, (BLOCK, 2 * HEAD_DIM), 1)
    first = lane < HEAD_DIM
    zero = jnp.zeros((BLOCK, 2 * HEAD_DIM), BF)
    paired = jnp.zeros((BLOCK, BLOCK), F32)
    chan = lax.broadcasted_iota(jnp.int32, (1, 2 * HEAD_DIM), 1)
    for pair in range(heads // 2):
        cut = slice(pair * 2 * HEAD_DIM, (pair + 1) * 2 * HEAD_DIM)
        u, g = driven[:, cut], dy_ref[:, cut]
        made = []
        for side in range(2):
            h = 2 * pair + side
            spread = cumul_t[:, h : h + 1] - cumul[h : h + 1, :]
            weights = jnp.exp(jnp.where(causal, spread, -1e30))
            mixed = (weights * scores).astype(BF)
            own = first if side == 0 else jnp.logical_not(first)
            raw = dg(jnp.where(own, g, zero), u, 1, 1)
            paired = paired + (weights * raw).astype(BF).astype(F32)
            made.append((dg(mixed, u, 1, 0), dg(mixed, g, 0, 0)))
        gain = jnp.where(chan < HEAD_DIM, gain_ref[2 * pair], gain_ref[2 * pair + 1])
        out_ref[:, cut] = jnp.where(first, made[0][0], made[1][0]) + gain * x_ref[:, cut].astype(F32)
        grad_ref[:, cut] = (
            jnp.where(first, made[0][1], made[1][1]) * delta_x[:, cut] + gain * g.astype(F32)
        )
    sums_ref[:, 0:STATE] = split_dot(paired, c, 0, 0)
    sums_ref[:, STATE:] = split_dot(paired, b, 1, 0)


def finish_kernel(
    bc_ref, in_ref, out_in, grad_in, sums_in, td_ref, gd_ref, grow_ref, dt_ref, out_ref, grad_ref, sums_ref
):
    b, c = both(bc_ref)
    width = out_in.shape[1]
    heads = width // HEAD_DIM
    growth_x, scale_x = expand(grow_ref[...], heads), expand(dt_ref[...], heads)
    state = in_ref[:, 0:16, :].reshape(width, STATE)
    adjoint = in_ref[:, 16:32, :].reshape(width, STATE)
    shape = sums_ref.shape[:2] + (STATE,)
    b_sum = sums_in[:, 0:STATE] + dg(td_ref[0], adjoint, 1, 0) + dg(td_ref[1], adjoint, 1, 0)
    c_sum = sums_in[:, STATE:] + dg(gd_ref[0], state, 1, 0) + dg(gd_ref[1], state, 1, 0)
    sums_ref[:, :, 0:STATE] = b_sum.astype(BF).reshape(shape)
    sums_ref[:, :, STATE:] = c_sum.astype(BF).reshape(shape)
    out_ref[...] = (out_in[...] + growth_x * dg(c, state, 1, 1)).astype(BF)
    grad_ref[...] = (grad_in[...] + scale_x * dg(b, adjoint, 1, 1)).astype(BF)


def total_kernel(got_ref, b_ref, c_ref):
    acc = got_ref[0].astype(F32)
    for k in range(1, got_ref.shape[0]):
        acc = acc + got_ref[k].astype(F32)
    b_ref[...] = acc[:, 0:STATE]
    c_ref[...] = acc[:, STATE:]


def exchange(x, axis):
    return lax.all_to_all(x, axis, 0, 0, tiled=True)


def near(x):
    return pltpu.with_memory_space_constraint(x, pltpu.VMEM)


def kernel(body, name, outs, *args, scalars=(), far=(), kept=True):
    args = [x if i in scalars or i in far else near(x) for i, x in enumerate(args)]
    specs = [
        pl.BlockSpec(memory_space=pltpu.SMEM if i in scalars else pltpu.VMEM)
        for i in range(len(args))
    ]
    shapes = tuple(
        pltpu.VMEM(s, d) if kept else jax.ShapeDtypeStruct(s, d) for s, d in outs
    )
    got = pl.pallas_call(
        body,
        out_shape=shapes,
        in_specs=specs,
        out_specs=tuple(pl.BlockSpec(memory_space=pltpu.VMEM) for _ in outs),
        compiler_params=pltpu.CompilerParams(vmem_limit_bytes=16 << 20),
        name=name,
    )(*args)
    return got if len(outs) > 1 else got[0]


def local(x_in, b_in, c_in, decay_codes, decay_rate, skip_gain, out_grad):
    seqs, groups = lax.axis_size("seq"), lax.axis_size("head")
    rows = b_in.shape[0]
    heads, tokens = decay_codes.shape
    wide = x_in.shape
    mine = jnp.concatenate([b_in, c_in], axis=0)
    bc = exchange(jnp.broadcast_to(mine[None], (groups, 2 * rows, STATE)), "head")
    td, gd, grow, dt, e = kernel(
        prepare_kernel,
        "prepare",
        [
            ((2,) + wide, BF),
            ((2,) + wide, BF),
            ((3 * heads, tokens), BF),
            ((3 * heads, tokens), BF),
            ((heads, 8, STATE), BF),
        ],
        x_in,
        out_grad,
        decay_codes,
        decay_rate,
        scalars=(3,),
        far=(0, 1, 2),
    )
    send = kernel(summary_kernel, "summary", [((seqs, 40, STATE), BF)], bc, td, gd, e)
    got = exchange(send, "seq")
    out_part, grad_part, sums_part = kernel(
        within_kernel,
        "within",
        [(wide, F32), (wide, F32), ((tokens, 2 * STATE), F32)],
        bc,
        x_in,
        out_grad,
        decay_codes,
        decay_rate,
        skip_gain,
        scalars=(4, 5),
        far=(1, 2, 3),
    )
    back = kernel(scan_kernel, "scan", [((seqs, 32, STATE), BF)], got)
    carried = exchange(back, "seq")
    ssm_out, input_grad, sums = kernel(
        finish_kernel,
        "finish",
        [(wide, BF), (wide, BF), ((groups, rows, 2 * STATE), BF)],
        bc,
        carried,
        out_part,
        grad_part,
        sums_part,
        td,
        gd,
        grow,
        dt,
    )
    grad_b, grad_c = kernel(
        total_kernel,
        "total",
        [((rows, STATE), F32)] * 2,
        exchange(sums, "head"),
        kept=False,
    )
    return ssm_out, input_grad, grad_b, grad_c


def solution(mesh):
    placed = (
        P("seq", "head"),
        P(("seq", "head"), None),
        P(("seq", "head"), None),
        P("head", "seq"),
        P("head"),
        P("head"),
        P("seq", "head"),
    )
    return jax.shard_map(
        local,
        mesh=mesh,
        in_specs=placed,
        out_specs=(
            P("seq", "head"),
            P("seq", "head"),
            P(("seq", "head"), None),
            P(("seq", "head"), None),
        ),
        check_vma=False,
    )
```

```python
import jax
import jax.numpy as jnp
from jax import lax
from jax.experimental import pallas as pl
from jax.experimental.pallas import tpu as pltpu
from jax.sharding import PartitionSpec as P

HEAD_DIM = 64
STATE = 128
BLOCK = 256
BF = jnp.bfloat16
F32 = jnp.float32
HEAD_START = 8
SEQ_START = 20


def turned(count, start):
    start = start if start < count else 0
    return [(k + start) % count for k in range(count)]


def dg(a, b, ca, cb):
    return lax.dot_general(a, b, (((ca,), (cb,)), ((), ())), preferred_element_type=F32)


def pieces(v, count):
    out = []
    for _ in range(count):
        part = v.astype(BF)
        out.append(part)
        v = v - part.astype(F32)
    return out


def split_dot(v, b, ca, cb):
    hi, lo = pieces(v, 2)
    return dg(hi, b, ca, cb) + dg(lo, b, ca, cb)


def stack(rows, count):
    return jnp.concatenate([p.astype(F32) for p in pieces(rows, count)], axis=0).astype(BF)


def expand(stacked, heads):
    shape = (stacked.shape[0], heads * HEAD_DIM)
    row = lax.broadcasted_iota(jnp.int32, shape, 0) % heads
    col = lax.broadcasted_iota(jnp.int32, shape, 1) // HEAD_DIM
    pick = jnp.where(row == col, 1.0, 0.0).astype(BF)
    return dg(stacked, pick, 0, 0)


def decode(codes, rate_ref):
    heads, tokens = codes.shape
    head = lax.broadcasted_iota(jnp.int32, (heads, tokens), 0)
    rate = jnp.zeros((heads, tokens), F32)
    for h in range(heads):
        rate = jnp.where(head == h, rate_ref[h], rate)
    delta = 0.5 + (codes & 1023).astype(F32) / 1024.0
    log_decay = -rate * delta - 0.1 * (codes >> 10).astype(F32)
    return delta, log_decay


def running_sum(log_decay):
    tokens = log_decay.shape[1]
    i = lax.broadcasted_iota(jnp.int32, (tokens, tokens), 0)
    j = lax.broadcasted_iota(jnp.int32, (tokens, tokens), 1)
    upper = jnp.where(i <= j, 1.0, 0.0).astype(BF)
    return sum(dg(p, upper, 1, 0) for p in pieces(log_decay, 3)[::-1])


def both(bc_ref):
    groups, half = bc_ref.shape[0], bc_ref.shape[1] // 2
    order = turned(groups, HEAD_START)
    b, c = [
        jnp.concatenate([bc_ref[order.index(g), rows, :] for g in range(groups)], axis=0)
        for rows in (slice(0, half), slice(half, 2 * half))
    ]
    return b, c


def prepare_kernel(x_ref, dy_ref, codes_ref, rate_ref, td_ref, gd_ref, grow_ref, dt_ref, e_ref):
    delta, log_decay = decode(codes_ref[...], rate_ref)
    cumul = running_sum(log_decay)
    heads = delta.shape[0]
    total = cumul[:, BLOCK - 1 :]
    growth = stack(jnp.exp(cumul), 3)
    tail = jnp.exp(total - cumul)
    driven = (x_ref[...].astype(F32) * expand(stack(delta, 2), heads)).astype(BF)
    td_ref[0], td_ref[1] = pieces(driven.astype(F32) * expand(stack(tail, 3), heads), 2)
    gd_ref[0], gd_ref[1] = pieces(dy_ref[...].astype(F32) * expand(growth, heads), 2)
    grow_ref[...] = growth
    dt_ref[...] = stack(delta * tail, 3)
    hi, mid, low = [p.astype(F32) for p in pieces(jnp.exp(total), 3)]
    row = lax.broadcasted_iota(jnp.int32, (8, STATE), 0)
    for h in range(heads):
        e_ref[h] = jnp.where(
            row == 0, hi[h : h + 1, :], jnp.where(row == 1, mid[h : h + 1, :], low[h : h + 1, :])
        ).astype(BF)


def summary_kernel(bc_ref, td_ref, gd_ref, e_ref, send_ref):
    b, c = both(bc_ref)
    parts, heads = send_ref.shape[0], e_ref.shape[0]
    state = dg(td_ref[0], b, 0, 0) + dg(td_ref[1], b, 0, 0)
    adjoint = dg(gd_ref[0], c, 0, 0) + dg(gd_ref[1], c, 0, 0)
    send_ref[:, 0:16, :] = state.astype(BF).reshape(parts, 16, STATE)
    send_ref[:, 16:32, :] = adjoint.astype(BF).reshape(parts, 16, STATE)
    per = parts // heads
    for h in range(heads):
        for q in range(per):
            send_ref[h * per + q, 32:40, :] = e_ref[h]


def scan_kernel(got_ref, send_ref):
    count = got_ref.shape[0]
    order = turned(count, SEQ_START)
    slots = [order.index(k) for k in range(count)]
    decays = {}
    for k in slots:
        tile = got_ref[k, 32:40, :].astype(F32)
        decays[k] = tile[0:1] + tile[1:2] + tile[2:3]
    run = jnp.zeros((16, STATE), F32)
    for k in slots:
        send_ref[k, 0:16, :] = run.astype(BF)
        run = decays[k] * run + got_ref[k, 0:16, :].astype(F32)
    run = jnp.zeros((16, STATE), F32)
    for k in slots[::-1]:
        send_ref[k, 16:32, :] = run.astype(BF)
        run = decays[k] * run + got_ref[k, 16:32, :].astype(F32)


def within_kernel(
    bc_ref, x_ref, dy_ref, codes_ref, rate_ref, gain_ref, out_ref, grad_ref, sums_ref
):
    b, c = both(bc_ref)
    delta, log_decay = decode(codes_ref[...], rate_ref)
    cumul = running_sum(log_decay)
    heads = cumul.shape[0]
    delta_x = expand(stack(delta, 2), heads)
    driven = (x_ref[...].astype(F32) * delta_x).astype(BF)
    i = lax.broadcasted_iota(jnp.int32, (BLOCK, BLOCK), 0)
    j = lax.broadcasted_iota(jnp.int32, (BLOCK, BLOCK), 1)
    causal = i >= j
    lower = jnp.where(causal, 1.0, 0.0).astype(BF)
    cumul_t = sum(dg(lower, p, 1, 1) for p in pieces(log_decay, 3)[::-1])
    scores = dg(c, b, 1, 1)
    lane = lax.broadcasted_iota(jnp.int32, (BLOCK, 2 * HEAD_DIM), 1)
    first = lane < HEAD_DIM
    zero = jnp.zeros((BLOCK, 2 * HEAD_DIM), BF)
    paired = jnp.zeros((BLOCK, BLOCK), F32)
    chan = lax.broadcasted_iota(jnp.int32, (1, 2 * HEAD_DIM), 1)
    for pair in range(heads // 2):
        cut = slice(pair * 2 * HEAD_DIM, (pair + 1) * 2 * HEAD_DIM)
        u, g = driven[:, cut], dy_ref[:, cut]
        made = []
        for side in range(2):
            h = 2 * pair + side
            spread = cumul_t[:, h : h + 1] - cumul[h : h + 1, :]
            weights = jnp.exp(jnp.where(causal, spread, -1e30))
            mixed = (weights * scores).astype(BF)
            own = first if side == 0 else jnp.logical_not(first)
            raw = dg(jnp.where(own, g, zero), u, 1, 1)
            paired = paired + (weights * raw).astype(BF).astype(F32)
            made.append((dg(mixed, u, 1, 0), dg(mixed, g, 0, 0)))
        gain = jnp.where(chan < HEAD_DIM, gain_ref[2 * pair], gain_ref[2 * pair + 1])
        out_ref[:, cut] = jnp.where(first, made[0][0], made[1][0]) + gain * x_ref[:, cut].astype(F32)
        grad_ref[:, cut] = (
            jnp.where(first, made[0][1], made[1][1]) * delta_x[:, cut] + gain * g.astype(F32)
        )
    sums_ref[:, 0:STATE] = split_dot(paired, c, 0, 0)
    sums_ref[:, STATE:] = split_dot(paired, b, 1, 0)


def sums_kernel(in_ref, sums_in, td_ref, gd_ref, sums_ref):
    width = td_ref.shape[2]
    state = in_ref[:, 0:16, :].reshape(width, STATE)
    adjoint = in_ref[:, 16:32, :].reshape(width, STATE)
    groups, rows = sums_ref.shape[:2]
    b_sum = sums_in[:, 0:STATE] + dg(td_ref[0], adjoint, 1, 0) + dg(td_ref[1], adjoint, 1, 0)
    c_sum = sums_in[:, STATE:] + dg(gd_ref[0], state, 1, 0) + dg(gd_ref[1], state, 1, 0)
    for slot, g in enumerate(turned(groups, HEAD_START)):
        sums_ref[slot, :, 0:STATE] = b_sum[g * rows : (g + 1) * rows].astype(BF)
        sums_ref[slot, :, STATE:] = c_sum[g * rows : (g + 1) * rows].astype(BF)


def finish_kernel(bc_ref, in_ref, out_in, grad_in, grow_ref, dt_ref, out_ref, grad_ref):
    b, c = both(bc_ref)
    width = out_in.shape[1]
    heads = width // HEAD_DIM
    state = in_ref[:, 0:16, :].reshape(width, STATE)
    adjoint = in_ref[:, 16:32, :].reshape(width, STATE)
    out_ref[...] = (out_in[...] + expand(grow_ref[...], heads) * dg(c, state, 1, 1)).astype(BF)
    grad_ref[...] = (grad_in[...] + expand(dt_ref[...], heads) * dg(b, adjoint, 1, 1)).astype(BF)


def total_kernel(got_ref, b_ref, c_ref):
    acc = got_ref[0].astype(F32)
    for k in range(1, got_ref.shape[0]):
        acc = acc + got_ref[k].astype(F32)
    b_ref[...] = acc[:, 0:STATE]
    c_ref[...] = acc[:, STATE:]


def exchange(x, axis):
    count = lax.axis_size(axis)
    order = turned(count, HEAD_START if axis == "head" else SEQ_START)
    return lax.all_to_all(x, axis, 0, 0, tiled=True, axis_index_groups=[order])


def near(x):
    return pltpu.with_memory_space_constraint(x, pltpu.VMEM)


def kernel(body, name, outs, *args, scalars=(), far=(), kept=True):
    args = [x if i in scalars or i in far else near(x) for i, x in enumerate(args)]
    specs = [
        pl.BlockSpec(memory_space=pltpu.SMEM if i in scalars else pltpu.VMEM)
        for i in range(len(args))
    ]
    shapes = tuple(
        pltpu.VMEM(s, d) if kept else jax.ShapeDtypeStruct(s, d) for s, d in outs
    )
    got = pl.pallas_call(
        body,
        out_shape=shapes,
        in_specs=specs,
        out_specs=tuple(pl.BlockSpec(memory_space=pltpu.VMEM) for _ in outs),
        compiler_params=pltpu.CompilerParams(vmem_limit_bytes=16 << 20),
        name=name,
    )(*args)
    return got if len(outs) > 1 else got[0]


def local(x_in, b_in, c_in, decay_codes, decay_rate, skip_gain, out_grad):
    seqs, groups = lax.axis_size("seq"), lax.axis_size("head")
    rows = b_in.shape[0]
    heads, tokens = decay_codes.shape
    wide = x_in.shape
    mine = jnp.concatenate([b_in, c_in], axis=0)
    bc = exchange(jnp.broadcast_to(mine[None], (groups, 2 * rows, STATE)), "head")
    td, gd, grow, dt, e = kernel(
        prepare_kernel,
        "prepare",
        [
            ((2,) + wide, BF),
            ((2,) + wide, BF),
            ((3 * heads, tokens), BF),
            ((3 * heads, tokens), BF),
            ((heads, 8, STATE), BF),
        ],
        x_in,
        out_grad,
        decay_codes,
        decay_rate,
        scalars=(3,),
        far=(0, 1, 2),
    )
    send = kernel(summary_kernel, "summary", [((seqs, 40, STATE), BF)], bc, td, gd, e)
    got = exchange(send, "seq")
    out_part, grad_part, sums_part = kernel(
        within_kernel,
        "within",
        [(wide, F32), (wide, F32), ((tokens, 2 * STATE), F32)],
        bc,
        x_in,
        out_grad,
        decay_codes,
        decay_rate,
        skip_gain,
        scalars=(4, 5),
        far=(1, 2, 3),
    )
    back = kernel(scan_kernel, "scan", [((seqs, 32, STATE), BF)], got)
    carried = exchange(back, "seq")
    sums = kernel(
        sums_kernel, "sums", [((groups, rows, 2 * STATE), BF)], carried, sums_part, td, gd
    )
    totals = exchange(sums, "head")
    ssm_out, input_grad = kernel(
        finish_kernel,
        "finish",
        [(wide, BF), (wide, BF)],
        bc,
        carried,
        out_part,
        grad_part,
        grow,
        dt,
    )
    grad_b, grad_c = kernel(
        total_kernel, "total", [((rows, STATE), F32)] * 2, totals, kept=False
    )
    return ssm_out, input_grad, grad_b, grad_c


def solution(mesh):
    placed = (
        P("seq", "head"),
        P(("seq", "head"), None),
        P(("seq", "head"), None),
        P("head", "seq"),
        P("head"),
        P("head"),
        P("seq", "head"),
    )
    return jax.shard_map(
        local,
        mesh=mesh,
        in_specs=placed,
        out_specs=(
            P("seq", "head"),
            P("seq", "head"),
            P(("seq", "head"), None),
            P(("seq", "head"), None),
        ),
        check_vma=False,
    )
```

```python
import jax
import jax.numpy as jnp
from jax import lax
from jax.experimental import pallas as pl
from jax.experimental.pallas import tpu as pltpu
from jax.sharding import PartitionSpec as P

HEAD_DIM = 64
STATE = 128
BLOCK = 256
BF = jnp.bfloat16
F32 = jnp.float32
HEAD_START = 8
SEQ_START = 20


def turned(count, start):
    start = start if start < count else 0
    return [(k + start) % count for k in range(count)]


def dg(a, b, ca, cb):
    return lax.dot_general(a, b, (((ca,), (cb,)), ((), ())), preferred_element_type=F32)


def pieces(v, count):
    out = []
    for _ in range(count):
        part = v.astype(BF)
        out.append(part)
        v = v - part.astype(F32)
    return out


def split_dot(v, b, ca, cb):
    hi, lo = pieces(v, 2)
    return dg(hi, b, ca, cb) + dg(lo, b, ca, cb)


def stack(rows, count):
    return jnp.concatenate([p.astype(F32) for p in pieces(rows, count)], axis=0).astype(BF)


def expand(stacked, heads):
    shape = (stacked.shape[0], heads * HEAD_DIM)
    row = lax.broadcasted_iota(jnp.int32, shape, 0) % heads
    col = lax.broadcasted_iota(jnp.int32, shape, 1) // HEAD_DIM
    pick = jnp.where(row == col, 1.0, 0.0).astype(BF)
    return dg(stacked, pick, 0, 0)


def decode(codes, rate_ref):
    heads, tokens = codes.shape
    head = lax.broadcasted_iota(jnp.int32, (heads, tokens), 0)
    rate = jnp.zeros((heads, tokens), F32)
    for h in range(heads):
        rate = jnp.where(head == h, rate_ref[h], rate)
    delta = 0.5 + (codes & 1023).astype(F32) / 1024.0
    log_decay = -rate * delta - 0.1 * (codes >> 10).astype(F32)
    return delta, log_decay


def running_sum(log_decay):
    tokens = log_decay.shape[1]
    i = lax.broadcasted_iota(jnp.int32, (tokens, tokens), 0)
    j = lax.broadcasted_iota(jnp.int32, (tokens, tokens), 1)
    upper = jnp.where(i <= j, 1.0, 0.0).astype(BF)
    return sum(dg(p, upper, 1, 0) for p in pieces(log_decay, 3)[::-1])


def both(bc_ref):
    groups, half = bc_ref.shape[0], bc_ref.shape[1] // 2
    order = turned(groups, HEAD_START)
    b, c = [
        jnp.concatenate([bc_ref[order.index(g), rows, :] for g in range(groups)], axis=0)
        for rows in (slice(0, half), slice(half, 2 * half))
    ]
    return b, c


def causal_mask():
    i = lax.broadcasted_iota(jnp.int32, (BLOCK, BLOCK), 0)
    j = lax.broadcasted_iota(jnp.int32, (BLOCK, BLOCK), 1)
    return i >= j


def weight_maker(log_decay, cumul):
    causal = causal_mask()
    lower = jnp.where(causal, 1.0, 0.0).astype(BF)
    cumul_t = sum(dg(lower, p, 1, 1) for p in pieces(log_decay, 3)[::-1])

    def weights(h):
        spread = cumul_t[:, h : h + 1] - cumul[h : h + 1, :]
        return jnp.exp(jnp.where(causal, spread, -1e30))

    return weights


def pair_cut(pair):
    return slice(pair * 2 * HEAD_DIM, (pair + 1) * 2 * HEAD_DIM)


def first_half():
    return lax.broadcasted_iota(jnp.int32, (BLOCK, 2 * HEAD_DIM), 1) < HEAD_DIM


def prepare_kernel(
    x_ref, dy_ref, codes_ref, rate_ref, td_ref, gd_ref, pr_ref, grow_ref, dt_ref, e_ref
):
    delta, log_decay = decode(codes_ref[...], rate_ref)
    cumul = running_sum(log_decay)
    heads = delta.shape[0]
    total = cumul[:, BLOCK - 1 :]
    growth = stack(jnp.exp(cumul), 3)
    tail = jnp.exp(total - cumul)
    driven = (x_ref[...].astype(F32) * expand(stack(delta, 2), heads)).astype(BF)
    td_ref[0], td_ref[1] = pieces(driven.astype(F32) * expand(stack(tail, 3), heads), 2)
    gd_ref[0], gd_ref[1] = pieces(dy_ref[...].astype(F32) * expand(growth, heads), 2)
    grow_ref[...] = growth
    dt_ref[...] = stack(delta * tail, 3)
    weights = weight_maker(log_decay, cumul)
    first = first_half()
    zero = jnp.zeros((BLOCK, 2 * HEAD_DIM), BF)
    paired = jnp.zeros((BLOCK, BLOCK), F32)
    for pair in range(heads // 2):
        u, g = driven[:, pair_cut(pair)], dy_ref[:, pair_cut(pair)]
        for side in range(2):
            own = first if side == 0 else jnp.logical_not(first)
            raw = dg(jnp.where(own, g, zero), u, 1, 1)
            paired = paired + (weights(2 * pair + side) * raw).astype(BF).astype(F32)
    pr_ref[0], pr_ref[1] = pieces(paired.T, 2)
    pr_ref[2], pr_ref[3] = pieces(paired, 2)
    hi, mid, low = [p.astype(F32) for p in pieces(jnp.exp(total), 3)]
    row = lax.broadcasted_iota(jnp.int32, (8, STATE), 0)
    for h in range(heads):
        e_ref[h] = jnp.where(
            row == 0, hi[h : h + 1, :], jnp.where(row == 1, mid[h : h + 1, :], low[h : h + 1, :])
        ).astype(BF)


def summary_kernel(bc_ref, td_ref, gd_ref, e_ref, send_ref):
    b, c = both(bc_ref)
    parts, heads = send_ref.shape[0], e_ref.shape[0]
    state = dg(td_ref[0], b, 0, 0) + dg(td_ref[1], b, 0, 0)
    adjoint = dg(gd_ref[0], c, 0, 0) + dg(gd_ref[1], c, 0, 0)
    send_ref[:, 0:16, :] = state.astype(BF).reshape(parts, 16, STATE)
    send_ref[:, 16:32, :] = adjoint.astype(BF).reshape(parts, 16, STATE)
    per = parts // heads
    for h in range(heads):
        for q in range(per):
            send_ref[h * per + q, 32:40, :] = e_ref[h]


def scan_kernel(got_ref, send_ref):
    count = got_ref.shape[0]
    order = turned(count, SEQ_START)
    slots = [order.index(k) for k in range(count)]
    decays = {}
    for k in slots:
        tile = got_ref[k, 32:40, :].astype(F32)
        decays[k] = tile[0:1] + tile[1:2] + tile[2:3]
    ahead = behind = jnp.zeros((16, STATE), F32)
    for k, m in zip(slots, slots[::-1]):
        send_ref[k, 0:16, :] = ahead.astype(BF)
        send_ref[m, 16:32, :] = behind.astype(BF)
        ahead = decays[k] * ahead + got_ref[k, 0:16, :].astype(F32)
        behind = decays[m] * behind + got_ref[m, 16:32, :].astype(F32)


def sums_kernel(bc_ref, in_ref, pr_ref, td_ref, gd_ref, sums_ref):
    b, c = both(bc_ref)
    width = td_ref.shape[2]
    groups, rows = sums_ref.shape[0], sums_ref.shape[1] // 2
    order = turned(groups, HEAD_START)
    for side, (parts, other) in enumerate(((td_ref, c), (gd_ref, b))):
        carry = in_ref[:, 16 - 16 * side : 32 - 16 * side, :].reshape(width, STATE)
        made = dg(pr_ref[2 * side], other, 1, 0) + dg(pr_ref[2 * side + 1], other, 1, 0)
        made = (made + dg(parts[0], carry, 1, 0) + dg(parts[1], carry, 1, 0)).astype(BF)
        for slot, g in enumerate(order):
            sums_ref[slot, side * rows : (side + 1) * rows, :] = made[g * rows : (g + 1) * rows]


def finish_kernel(
    bc_ref, in_ref, grow_ref, dt_ref, x_ref, dy_ref, codes_ref, rate_ref, gain_ref, out_ref, grad_ref
):
    b, c = both(bc_ref)
    delta, log_decay = decode(codes_ref[...], rate_ref)
    cumul = running_sum(log_decay)
    heads = delta.shape[0]
    width = heads * HEAD_DIM
    delta_x = expand(stack(delta, 2), heads)
    driven = (x_ref[...].astype(F32) * delta_x).astype(BF)
    state = in_ref[:, 0:16, :].reshape(width, STATE)
    adjoint = in_ref[:, 16:32, :].reshape(width, STATE)
    out_cross = expand(grow_ref[...], heads) * dg(c, state, 1, 1)
    grad_cross = expand(dt_ref[...], heads) * dg(b, adjoint, 1, 1)
    scores = dg(c, b, 1, 1)
    weights = weight_maker(log_decay, cumul)
    first = first_half()
    chan = lax.broadcasted_iota(jnp.int32, (1, 2 * HEAD_DIM), 1)
    for pair in range(heads // 2):
        cut = pair_cut(pair)
        u, g = driven[:, cut], dy_ref[:, cut]
        made = []
        for side in range(2):
            mixed = (weights(2 * pair + side) * scores).astype(BF)
            made.append((dg(mixed, u, 1, 0), dg(mixed, g, 0, 0)))
        gain = jnp.where(chan < HEAD_DIM, gain_ref[2 * pair], gain_ref[2 * pair + 1])
        out = jnp.where(first, made[0][0], made[1][0]) + out_cross[:, cut]
        grad = jnp.where(first, made[0][1], made[1][1]) * delta_x[:, cut] + grad_cross[:, cut]
        out_ref[:, cut] = (out + gain * x_ref[:, cut].astype(F32)).astype(BF)
        grad_ref[:, cut] = (grad + gain * g.astype(F32)).astype(BF)


def total_kernel(got_ref, b_ref, c_ref):
    acc = got_ref[0].astype(F32)
    for k in range(1, got_ref.shape[0]):
        acc = acc + got_ref[k].astype(F32)
    rows = b_ref.shape[0]
    b_ref[...] = acc[0:rows]
    c_ref[...] = acc[rows:]


def exchange(x, axis):
    count = lax.axis_size(axis)
    order = turned(count, HEAD_START if axis == "head" else SEQ_START)
    return lax.all_to_all(x, axis, 0, 0, tiled=True, axis_index_groups=[order])


def near(x):
    return pltpu.with_memory_space_constraint(x, pltpu.VMEM)


def kernel(body, name, outs, *args, scalars=(), far=(), kept=True):
    args = [x if i in scalars or i in far else near(x) for i, x in enumerate(args)]
    specs = [
        pl.BlockSpec(memory_space=pltpu.SMEM if i in scalars else pltpu.VMEM)
        for i in range(len(args))
    ]
    shapes = tuple(
        pltpu.VMEM(s, d) if kept else jax.ShapeDtypeStruct(s, d) for s, d in outs
    )
    got = pl.pallas_call(
        body,
        out_shape=shapes,
        in_specs=specs,
        out_specs=tuple(pl.BlockSpec(memory_space=pltpu.VMEM) for _ in outs),
        compiler_params=pltpu.CompilerParams(vmem_limit_bytes=16 << 20),
        name=name,
    )(*args)
    return got if len(outs) > 1 else got[0]


def local(x_in, b_in, c_in, decay_codes, decay_rate, skip_gain, out_grad):
    seqs, groups = lax.axis_size("seq"), lax.axis_size("head")
    rows = b_in.shape[0]
    heads, tokens = decay_codes.shape
    wide = x_in.shape
    mine = jnp.concatenate([b_in, c_in], axis=0)
    bc = exchange(jnp.broadcast_to(mine[None], (groups, 2 * rows, STATE)), "head")
    td, gd, paired, grow, dt, e = kernel(
        prepare_kernel,
        "prepare",
        [
            ((2,) + wide, BF),
            ((2,) + wide, BF),
            ((4, tokens, tokens), BF),
            ((3 * heads, tokens), BF),
            ((3 * heads, tokens), BF),
            ((heads, 8, STATE), BF),
        ],
        x_in,
        out_grad,
        decay_codes,
        decay_rate,
        scalars=(3,),
        far=(0, 1, 2),
    )
    send = kernel(summary_kernel, "summary", [((seqs, 40, STATE), BF)], bc, td, gd, e)
    got = exchange(send, "seq")
    back = kernel(scan_kernel, "scan", [((seqs, 32, STATE), BF)], got)
    carried = exchange(back, "seq")
    sums = kernel(
        sums_kernel, "sums", [((groups, 2 * rows, STATE), BF)], bc, carried, paired, td, gd
    )
    totals = exchange(sums, "head")
    ssm_out, input_grad = kernel(
        finish_kernel,
        "finish",
        [(wide, BF), (wide, BF)],
        bc,
        carried,
        grow,
        dt,
        x_in,
        out_grad,
        decay_codes,
        decay_rate,
        skip_gain,
        scalars=(7, 8),
        far=(4, 5, 6),
    )
    grad_b, grad_c = kernel(
        total_kernel, "total", [((rows, STATE), F32)] * 2, totals, kept=False
    )
    return ssm_out, input_grad, grad_b, grad_c


def solution(mesh):
    placed = (
        P("seq", "head"),
        P(("seq", "head"), None),
        P(("seq", "head"), None),
        P("head", "seq"),
        P("head"),
        P("head"),
        P("seq", "head"),
    )
    return jax.shard_map(
        local,
        mesh=mesh,
        in_specs=placed,
        out_specs=(
            P("seq", "head"),
            P("seq", "head"),
            P(("seq", "head"), None),
            P(("seq", "head"), None),
        ),
        check_vma=False,
    )
```

```python
import jax
import jax.numpy as jnp
from jax import lax
from jax.experimental import pallas as pl
from jax.experimental.pallas import tpu as pltpu
from jax.sharding import PartitionSpec as P

HEAD_DIM = 64
STATE = 128
BLOCK = 256
BF = jnp.bfloat16
F32 = jnp.float32
HEAD_START = 8
SEQ_START = 20


def turned(count, start):
    start = start if start < count else 0
    return [(k + start) % count for k in range(count)]


def dg(a, b, ca, cb):
    return lax.dot_general(a, b, (((ca,), (cb,)), ((), ())), preferred_element_type=F32)


def pieces(v, count):
    out = []
    for _ in range(count):
        part = v.astype(BF)
        out.append(part)
        v = v - part.astype(F32)
    return out


def split_dot(v, b, ca, cb):
    hi, lo = pieces(v, 2)
    return dg(hi, b, ca, cb) + dg(lo, b, ca, cb)


def stack(rows, count):
    return jnp.concatenate([p.astype(F32) for p in pieces(rows, count)], axis=0).astype(BF)


def expand(stacked, heads):
    shape = (stacked.shape[0], heads * HEAD_DIM)
    row = lax.broadcasted_iota(jnp.int32, shape, 0) % heads
    col = lax.broadcasted_iota(jnp.int32, shape, 1) // HEAD_DIM
    pick = jnp.where(row == col, 1.0, 0.0).astype(BF)
    return dg(stacked, pick, 0, 0)


def decode(codes, rate_ref):
    heads, tokens = codes.shape
    head = lax.broadcasted_iota(jnp.int32, (heads, tokens), 0)
    rate = jnp.zeros((heads, tokens), F32)
    for h in range(heads):
        rate = jnp.where(head == h, rate_ref[h], rate)
    delta = 0.5 + (codes & 1023).astype(F32) / 1024.0
    log_decay = -rate * delta - 0.1 * (codes >> 10).astype(F32)
    return delta, log_decay


def running_sum(log_decay):
    tokens = log_decay.shape[1]
    i = lax.broadcasted_iota(jnp.int32, (tokens, tokens), 0)
    j = lax.broadcasted_iota(jnp.int32, (tokens, tokens), 1)
    upper = jnp.where(i <= j, 1.0, 0.0).astype(BF)
    return sum(dg(p, upper, 1, 0) for p in pieces(log_decay, 3)[::-1])


def both(bc_ref):
    groups, half = bc_ref.shape[0], bc_ref.shape[1] // 2
    order = turned(groups, HEAD_START)
    b, c = [
        jnp.concatenate([bc_ref[order.index(g), rows, :] for g in range(groups)], axis=0)
        for rows in (slice(0, half), slice(half, 2 * half))
    ]
    return b, c


def causal_mask():
    i = lax.broadcasted_iota(jnp.int32, (BLOCK, BLOCK), 0)
    j = lax.broadcasted_iota(jnp.int32, (BLOCK, BLOCK), 1)
    return i >= j


def weight_maker(log_decay, cumul):
    causal = causal_mask()
    lower = jnp.where(causal, 1.0, 0.0).astype(BF)
    cumul_t = sum(dg(lower, p, 1, 1) for p in pieces(log_decay, 3)[::-1])

    def weights(h):
        spread = cumul_t[:, h : h + 1] - cumul[h : h + 1, :]
        return jnp.exp(jnp.where(causal, spread, -1e30))

    return weights


def pair_cut(pair):
    return slice(pair * 2 * HEAD_DIM, (pair + 1) * 2 * HEAD_DIM)


def first_half():
    return lax.broadcasted_iota(jnp.int32, (BLOCK, 2 * HEAD_DIM), 1) < HEAD_DIM


def prepare_kernel(
    x_ref, dy_ref, codes_ref, rate_ref, td_ref, gd_ref, pr_ref, grow_ref, dt_ref, e_ref
):
    delta, log_decay = decode(codes_ref[...], rate_ref)
    cumul = running_sum(log_decay)
    heads = delta.shape[0]
    total = cumul[:, BLOCK - 1 :]
    growth = stack(jnp.exp(cumul), 3)
    tail = jnp.exp(total - cumul)
    driven = (x_ref[...].astype(F32) * expand(stack(delta, 2), heads)).astype(BF)
    td_ref[0], td_ref[1] = pieces(driven.astype(F32) * expand(stack(tail, 3), heads), 2)
    gd_ref[0], gd_ref[1] = pieces(dy_ref[...].astype(F32) * expand(growth, heads), 2)
    grow_ref[...] = growth
    dt_ref[...] = stack(delta * tail, 3)
    weights = weight_maker(log_decay, cumul)
    first = first_half()
    zero = jnp.zeros((BLOCK, 2 * HEAD_DIM), BF)
    paired = jnp.zeros((BLOCK, BLOCK), F32)
    for pair in range(heads // 2):
        u, g = driven[:, pair_cut(pair)], dy_ref[:, pair_cut(pair)]
        for side in range(2):
            own = first if side == 0 else jnp.logical_not(first)
            raw = dg(jnp.where(own, g, zero), u, 1, 1)
            paired = paired + (weights(2 * pair + side) * raw).astype(BF).astype(F32)
    pr_ref[0], pr_ref[1] = pieces(paired.T, 2)
    pr_ref[2], pr_ref[3] = pieces(paired, 2)
    hi, mid, low = [p.astype(F32) for p in pieces(jnp.exp(total), 3)]
    row = lax.broadcasted_iota(jnp.int32, (8, STATE), 0)
    for h in range(heads):
        e_ref[h] = jnp.where(
            row == 0, hi[h : h + 1, :], jnp.where(row == 1, mid[h : h + 1, :], low[h : h + 1, :])
        ).astype(BF)


def summary_kernel(bc_ref, td_ref, gd_ref, e_ref, send_ref):
    b, c = both(bc_ref)
    parts, heads = send_ref.shape[0], e_ref.shape[0]
    state = dg(td_ref[0], b, 0, 0) + dg(td_ref[1], b, 0, 0)
    adjoint = dg(gd_ref[0], c, 0, 0) + dg(gd_ref[1], c, 0, 0)
    send_ref[:, 0:16, :] = state.astype(BF).reshape(parts, 16, STATE)
    send_ref[:, 16:32, :] = adjoint.astype(BF).reshape(parts, 16, STATE)
    per = parts // heads
    for h in range(heads):
        for q in range(per):
            send_ref[h * per + q, 32:40, :] = e_ref[h]


def scan_kernel(got_ref, send_ref):
    count = got_ref.shape[0]
    order = turned(count, SEQ_START)
    slots = [order.index(k) for k in range(count)]
    decays = {}
    for k in slots:
        tile = got_ref[k, 32:40, :].astype(F32)
        decays[k] = tile[0:1] + tile[1:2] + tile[2:3]
    ahead = behind = jnp.zeros((16, STATE), F32)
    for k, m in zip(slots, slots[::-1]):
        send_ref[k, 0:16, :] = ahead.astype(BF)
        send_ref[m, 16:32, :] = behind.astype(BF)
        ahead = decays[k] * ahead + got_ref[k, 0:16, :].astype(F32)
        behind = decays[m] * behind + got_ref[m, 16:32, :].astype(F32)


def sums_kernel(bc_ref, in_ref, pr_ref, td_ref, gd_ref, sums_ref):
    b, c = both(bc_ref)
    width = td_ref.shape[2]
    groups, rows = sums_ref.shape[0], sums_ref.shape[1] // 2
    order = turned(groups, HEAD_START)
    for side, (parts, other) in enumerate(((td_ref, c), (gd_ref, b))):
        carry = in_ref[:, 16 - 16 * side : 32 - 16 * side, :].reshape(width, STATE)
        made = dg(pr_ref[2 * side], other, 1, 0) + dg(pr_ref[2 * side + 1], other, 1, 0)
        made = (made + dg(parts[0], carry, 1, 0) + dg(parts[1], carry, 1, 0)).astype(BF)
        for slot, g in enumerate(order):
            sums_ref[slot, side * rows : (side + 1) * rows, :] = made[g * rows : (g + 1) * rows]


def finish_kernel(
    bc_ref, in_ref, grow_ref, dt_ref, x_ref, dy_ref, codes_ref, rate_ref, gain_ref, out_ref, grad_ref
):
    b, c = both(bc_ref)
    delta, log_decay = decode(codes_ref[...], rate_ref)
    cumul = running_sum(log_decay)
    heads = delta.shape[0]
    width = heads * HEAD_DIM
    delta_x = expand(stack(delta, 2), heads)
    driven = (x_ref[...].astype(F32) * delta_x).astype(BF)
    state = in_ref[:, 0:16, :].reshape(width, STATE)
    adjoint = in_ref[:, 16:32, :].reshape(width, STATE)
    out_cross = expand(grow_ref[...], heads) * dg(c, state, 1, 1)
    grad_cross = expand(dt_ref[...], heads) * dg(b, adjoint, 1, 1)
    scores = dg(c, b, 1, 1)
    weights = weight_maker(log_decay, cumul)
    first = first_half()
    chan = lax.broadcasted_iota(jnp.int32, (1, 2 * HEAD_DIM), 1)
    for pair in range(heads // 2):
        cut = pair_cut(pair)
        u, g = driven[:, cut], dy_ref[:, cut]
        made = []
        for side in range(2):
            mixed = (weights(2 * pair + side) * scores).astype(BF)
            made.append((dg(mixed, u, 1, 0), dg(mixed, g, 0, 0)))
        gain = jnp.where(chan < HEAD_DIM, gain_ref[2 * pair], gain_ref[2 * pair + 1])
        out = jnp.where(first, made[0][0], made[1][0]) + out_cross[:, cut]
        grad = jnp.where(first, made[0][1], made[1][1]) * delta_x[:, cut] + grad_cross[:, cut]
        out_ref[:, cut] = (out + gain * x_ref[:, cut].astype(F32)).astype(BF)
        grad_ref[:, cut] = (grad + gain * g.astype(F32)).astype(BF)


def total_kernel(got_ref, b_ref, c_ref):
    acc = got_ref[0].astype(F32)
    for k in range(1, got_ref.shape[0]):
        acc = acc + got_ref[k].astype(F32)
    rows = b_ref.shape[0]
    b_ref[...] = acc[0:rows]
    c_ref[...] = acc[rows:]


def exchange(x, axis):
    count = lax.axis_size(axis)
    order = turned(count, HEAD_START if axis == "head" else SEQ_START)
    return lax.all_to_all(x, axis, 0, 0, tiled=True, axis_index_groups=[order])


def near(x):
    return pltpu.with_memory_space_constraint(x, pltpu.VMEM)


def kernel(body, name, outs, *args, scalars=(), far=(), kept=True):
    args = [x if i in scalars or i in far else near(x) for i, x in enumerate(args)]
    specs = [
        pl.BlockSpec(memory_space=pltpu.SMEM if i in scalars else pltpu.VMEM)
        for i in range(len(args))
    ]
    shapes = tuple(
        pltpu.VMEM(s, d) if kept else jax.ShapeDtypeStruct(s, d) for s, d in outs
    )
    got = pl.pallas_call(
        body,
        out_shape=shapes,
        in_specs=specs,
        out_specs=tuple(pl.BlockSpec(memory_space=pltpu.VMEM) for _ in outs),
        compiler_params=pltpu.CompilerParams(vmem_limit_bytes=16 << 20),
        name=name,
    )(*args)
    return got if len(outs) > 1 else got[0]


def local(x_in, b_in, c_in, decay_codes, decay_rate, skip_gain, out_grad):
    seqs, groups = lax.axis_size("seq"), lax.axis_size("head")
    rows = b_in.shape[0]
    heads, tokens = decay_codes.shape
    wide = x_in.shape
    spread = [jnp.broadcast_to(v[None], (groups, rows, STATE)) for v in (b_in, c_in)]
    bc = exchange(jnp.concatenate(spread, axis=1), "head")
    td, gd, paired, grow, dt, e = kernel(
        prepare_kernel,
        "prepare",
        [
            ((2,) + wide, BF),
            ((2,) + wide, BF),
            ((4, tokens, tokens), BF),
            ((3 * heads, tokens), BF),
            ((3 * heads, tokens), BF),
            ((heads, 8, STATE), BF),
        ],
        x_in,
        out_grad,
        decay_codes,
        decay_rate,
        scalars=(3,),
        far=(0, 1, 2),
    )
    send = kernel(summary_kernel, "summary", [((seqs, 40, STATE), BF)], bc, td, gd, e)
    got = exchange(send, "seq")
    back = kernel(scan_kernel, "scan", [((seqs, 32, STATE), BF)], got)
    carried = exchange(back, "seq")
    sums = kernel(
        sums_kernel, "sums", [((groups, 2 * rows, STATE), BF)], bc, carried, paired, td, gd
    )
    totals = exchange(sums, "head")
    ssm_out, input_grad = kernel(
        finish_kernel,
        "finish",
        [(wide, BF), (wide, BF)],
        bc,
        carried,
        grow,
        dt,
        x_in,
        out_grad,
        decay_codes,
        decay_rate,
        skip_gain,
        scalars=(7, 8),
        far=(4, 5, 6),
    )
    grad_b, grad_c = kernel(
        total_kernel, "total", [((rows, STATE), F32)] * 2, totals, kept=False
    )
    return ssm_out, input_grad, grad_b, grad_c


def solution(mesh):
    placed = (
        P("seq", "head"),
        P(("seq", "head"), None),
        P(("seq", "head"), None),
        P("head", "seq"),
        P("head"),
        P("head"),
        P("seq", "head"),
    )
    return jax.shard_map(
        local,
        mesh=mesh,
        in_specs=placed,
        out_specs=(
            P("seq", "head"),
            P("seq", "head"),
            P(("seq", "head"), None),
            P(("seq", "head"), None),
        ),
        check_vma=False,
    )
```

```python
import jax
import jax.numpy as jnp
from jax import lax
from jax.experimental import pallas as pl
from jax.experimental.pallas import tpu as pltpu
from jax.sharding import PartitionSpec as P

HEAD_DIM = 64
STATE = 128
BLOCK = 256
BF = jnp.bfloat16
F32 = jnp.float32
HEAD_START = 8
SEQ_START = 20


def turned(count, start):
    start = start if start < count else 0
    return [(k + start) % count for k in range(count)]


def dg(a, b, ca, cb):
    return lax.dot_general(a, b, (((ca,), (cb,)), ((), ())), preferred_element_type=F32)


def pieces(v, count):
    out = []
    for _ in range(count):
        part = v.astype(BF)
        out.append(part)
        v = v - part.astype(F32)
    return out


def split_dot(v, b, ca, cb):
    hi, lo = pieces(v, 2)
    return dg(hi, b, ca, cb) + dg(lo, b, ca, cb)


def stack(rows, count):
    return jnp.concatenate([p.astype(F32) for p in pieces(rows, count)], axis=0).astype(BF)


def expand(stacked, heads):
    shape = (stacked.shape[0], heads * HEAD_DIM)
    row = lax.broadcasted_iota(jnp.int32, shape, 0) % heads
    col = lax.broadcasted_iota(jnp.int32, shape, 1) // HEAD_DIM
    pick = jnp.where(row == col, 1.0, 0.0).astype(BF)
    return dg(stacked, pick, 0, 0)


def decode(codes, rate_ref):
    heads, tokens = codes.shape
    head = lax.broadcasted_iota(jnp.int32, (heads, tokens), 0)
    rate = jnp.zeros((heads, tokens), F32)
    for h in range(heads):
        rate = jnp.where(head == h, rate_ref[h], rate)
    delta = 0.5 + (codes & 1023).astype(F32) / 1024.0
    log_decay = -rate * delta - 0.1 * (codes >> 10).astype(F32)
    return delta, log_decay


def running_sum(log_decay):
    tokens = log_decay.shape[1]
    i = lax.broadcasted_iota(jnp.int32, (tokens, tokens), 0)
    j = lax.broadcasted_iota(jnp.int32, (tokens, tokens), 1)
    upper = jnp.where(i <= j, 1.0, 0.0).astype(BF)
    return sum(dg(p, upper, 1, 0) for p in pieces(log_decay, 3)[::-1])


def both(bc_ref):
    groups, half = bc_ref.shape[0], bc_ref.shape[1] // 2
    order = turned(groups, HEAD_START)
    b, c = [
        jnp.concatenate([bc_ref[order.index(g), rows, :] for g in range(groups)], axis=0)
        for rows in (slice(0, half), slice(half, 2 * half))
    ]
    return b, c


def causal_mask():
    i = lax.broadcasted_iota(jnp.int32, (BLOCK, BLOCK), 0)
    j = lax.broadcasted_iota(jnp.int32, (BLOCK, BLOCK), 1)
    return i >= j


def weight_maker(log_decay, cumul):
    causal = causal_mask()
    lower = jnp.where(causal, 1.0, 0.0).astype(BF)
    cumul_t = sum(dg(lower, p, 1, 1) for p in pieces(log_decay, 3)[::-1])

    def weights(h):
        spread = cumul_t[:, h : h + 1] - cumul[h : h + 1, :]
        return jnp.exp(jnp.where(causal, spread, -1e30))

    return weights


def pair_cut(pair):
    return slice(pair * 2 * HEAD_DIM, (pair + 1) * 2 * HEAD_DIM)


def first_half():
    return lax.broadcasted_iota(jnp.int32, (BLOCK, 2 * HEAD_DIM), 1) < HEAD_DIM


def prepare_kernel(
    x_ref, dy_ref, codes_ref, rate_ref, td_ref, gd_ref, tt_ref, gt_ref, pr_ref, grow_ref, dt_ref, e_ref
):
    delta, log_decay = decode(codes_ref[...], rate_ref)
    cumul = running_sum(log_decay)
    heads = delta.shape[0]
    total = cumul[:, BLOCK - 1 :]
    growth = stack(jnp.exp(cumul), 3)
    tail = jnp.exp(total - cumul)
    driven = (x_ref[...].astype(F32) * expand(stack(delta, 2), heads)).astype(BF)
    for wide_ref, turned_ref, value in (
        (td_ref, tt_ref, driven.astype(F32) * expand(stack(tail, 3), heads)),
        (gd_ref, gt_ref, dy_ref[...].astype(F32) * expand(growth, heads)),
    ):
        for k, part in enumerate(pieces(value, 2)):
            width = part.shape[1]
            wide_ref[:, k * width : (k + 1) * width] = part
            turned_ref[:, k * BLOCK : (k + 1) * BLOCK] = part.T
    grow_ref[...] = growth
    dt_ref[...] = stack(delta * tail, 3)
    weights = weight_maker(log_decay, cumul)
    first = first_half()
    zero = jnp.zeros((BLOCK, 2 * HEAD_DIM), BF)
    paired = jnp.zeros((BLOCK, BLOCK), F32)
    for pair in range(heads // 2):
        u, g = driven[:, pair_cut(pair)], dy_ref[:, pair_cut(pair)]
        for side in range(2):
            own = first if side == 0 else jnp.logical_not(first)
            raw = dg(jnp.where(own, g, zero), u, 1, 1)
            paired = paired + (weights(2 * pair + side) * raw).astype(BF).astype(F32)
    for side, value in enumerate((paired.T, paired)):
        for k, part in enumerate(pieces(value, 2)):
            pr_ref[side, :, k * BLOCK : (k + 1) * BLOCK] = part
    hi, mid, low = [p.astype(F32) for p in pieces(jnp.exp(total), 3)]
    row = lax.broadcasted_iota(jnp.int32, (8, STATE), 0)
    for h in range(heads):
        e_ref[h] = jnp.where(
            row == 0, hi[h : h + 1, :], jnp.where(row == 1, mid[h : h + 1, :], low[h : h + 1, :])
        ).astype(BF)


def twice(v):
    return jnp.concatenate([v, v], axis=0)


def summary_kernel(bc_ref, tt_ref, gt_ref, e_ref, send_ref):
    b, c = both(bc_ref)
    parts, heads = send_ref.shape[0], e_ref.shape[0]
    state = dg(tt_ref[...], twice(b), 1, 0)
    adjoint = dg(gt_ref[...], twice(c), 1, 0)
    send_ref[:, 0:16, :] = state.astype(BF).reshape(parts, 16, STATE)
    send_ref[:, 16:32, :] = adjoint.astype(BF).reshape(parts, 16, STATE)
    per = parts // heads
    for h in range(heads):
        for q in range(per):
            send_ref[h * per + q, 32:40, :] = e_ref[h]


def scan_kernel(got_ref, send_ref):
    count = got_ref.shape[0]
    order = turned(count, SEQ_START)
    slots = [order.index(k) for k in range(count)]
    decays = {}
    for k in slots:
        tile = got_ref[k, 32:40, :].astype(F32)
        decays[k] = tile[0:1] + tile[1:2] + tile[2:3]
    ahead = behind = jnp.zeros((16, STATE), F32)
    for k, m in zip(slots, slots[::-1]):
        send_ref[k, 0:16, :] = ahead.astype(BF)
        send_ref[m, 16:32, :] = behind.astype(BF)
        ahead = decays[k] * ahead + got_ref[k, 0:16, :].astype(F32)
        behind = decays[m] * behind + got_ref[m, 16:32, :].astype(F32)


def sums_kernel(bc_ref, in_ref, pr_ref, td_ref, gd_ref, sums_ref):
    b, c = both(bc_ref)
    width = td_ref.shape[1] // 2
    groups, rows = sums_ref.shape[0], sums_ref.shape[1] // 2
    order = turned(groups, HEAD_START)
    for side, (parts, other) in enumerate(((td_ref, c), (gd_ref, b))):
        carry = in_ref[:, 16 - 16 * side : 32 - 16 * side, :].reshape(width, STATE)
        made = dg(pr_ref[side], twice(other), 1, 0) + dg(parts[...], twice(carry), 1, 0)
        made = made.astype(BF)
        for slot, g in enumerate(order):
            sums_ref[slot, side * rows : (side + 1) * rows, :] = made[g * rows : (g + 1) * rows]


def finish_kernel(
    bc_ref, in_ref, grow_ref, dt_ref, x_ref, dy_ref, codes_ref, rate_ref, gain_ref, out_ref, grad_ref
):
    b, c = both(bc_ref)
    delta, log_decay = decode(codes_ref[...], rate_ref)
    cumul = running_sum(log_decay)
    heads = delta.shape[0]
    width = heads * HEAD_DIM
    delta_x = expand(stack(delta, 2), heads)
    driven = (x_ref[...].astype(F32) * delta_x).astype(BF)
    state = in_ref[:, 0:16, :].reshape(width, STATE)
    adjoint = in_ref[:, 16:32, :].reshape(width, STATE)
    out_cross = expand(grow_ref[...], heads) * dg(c, state, 1, 1)
    grad_cross = expand(dt_ref[...], heads) * dg(b, adjoint, 1, 1)
    scores = dg(c, b, 1, 1)
    weights = weight_maker(log_decay, cumul)
    first = first_half()
    chan = lax.broadcasted_iota(jnp.int32, (1, 2 * HEAD_DIM), 1)
    for pair in range(heads // 2):
        cut = pair_cut(pair)
        u, g = driven[:, cut], dy_ref[:, cut]
        made = []
        for side in range(2):
            mixed = (weights(2 * pair + side) * scores).astype(BF)
            made.append((dg(mixed, u, 1, 0), dg(mixed, g, 0, 0)))
        gain = jnp.where(chan < HEAD_DIM, gain_ref[2 * pair], gain_ref[2 * pair + 1])
        out = jnp.where(first, made[0][0], made[1][0]) + out_cross[:, cut]
        grad = jnp.where(first, made[0][1], made[1][1]) * delta_x[:, cut] + grad_cross[:, cut]
        out_ref[:, cut] = (out + gain * x_ref[:, cut].astype(F32)).astype(BF)
        grad_ref[:, cut] = (grad + gain * g.astype(F32)).astype(BF)


def total_kernel(got_ref, b_ref, c_ref):
    acc = got_ref[0].astype(F32)
    for k in range(1, got_ref.shape[0]):
        acc = acc + got_ref[k].astype(F32)
    rows = b_ref.shape[0]
    b_ref[...] = acc[0:rows]
    c_ref[...] = acc[rows:]


def exchange(x, axis):
    count = lax.axis_size(axis)
    order = turned(count, HEAD_START if axis == "head" else SEQ_START)
    return lax.all_to_all(x, axis, 0, 0, tiled=True, axis_index_groups=[order])


def near(x):
    return pltpu.with_memory_space_constraint(x, pltpu.VMEM)


def kernel(body, name, outs, *args, scalars=(), far=(), kept=True):
    args = [x if i in scalars or i in far else near(x) for i, x in enumerate(args)]
    specs = [
        pl.BlockSpec(memory_space=pltpu.SMEM if i in scalars else pltpu.VMEM)
        for i in range(len(args))
    ]
    shapes = tuple(
        pltpu.VMEM(s, d) if kept else jax.ShapeDtypeStruct(s, d) for s, d in outs
    )
    got = pl.pallas_call(
        body,
        out_shape=shapes,
        in_specs=specs,
        out_specs=tuple(pl.BlockSpec(memory_space=pltpu.VMEM) for _ in outs),
        compiler_params=pltpu.CompilerParams(vmem_limit_bytes=16 << 20),
        name=name,
    )(*args)
    return got if len(outs) > 1 else got[0]


def local(x_in, b_in, c_in, decay_codes, decay_rate, skip_gain, out_grad):
    seqs, groups = lax.axis_size("seq"), lax.axis_size("head")
    rows = b_in.shape[0]
    heads, tokens = decay_codes.shape
    wide = x_in.shape
    spread = [jnp.broadcast_to(v[None], (groups, rows, STATE)) for v in (b_in, c_in)]
    bc = exchange(jnp.concatenate(spread, axis=1), "head")
    td, gd, tt, gt, paired, grow, dt, e = kernel(
        prepare_kernel,
        "prepare",
        [
            ((tokens, 2 * wide[1]), BF),
            ((tokens, 2 * wide[1]), BF),
            ((wide[1], 2 * tokens), BF),
            ((wide[1], 2 * tokens), BF),
            ((2, tokens, 2 * tokens), BF),
            ((3 * heads, tokens), BF),
            ((3 * heads, tokens), BF),
            ((heads, 8, STATE), BF),
        ],
        x_in,
        out_grad,
        decay_codes,
        decay_rate,
        scalars=(3,),
        far=(0, 1, 2),
    )
    send = kernel(summary_kernel, "summary", [((seqs, 40, STATE), BF)], bc, tt, gt, e)
    got = exchange(send, "seq")
    back = kernel(scan_kernel, "scan", [((seqs, 32, STATE), BF)], got)
    carried = exchange(back, "seq")
    sums = kernel(
        sums_kernel, "sums", [((groups, 2 * rows, STATE), BF)], bc, carried, paired, td, gd
    )
    totals = exchange(sums, "head")
    ssm_out, input_grad = kernel(
        finish_kernel,
        "finish",
        [(wide, BF), (wide, BF)],
        bc,
        carried,
        grow,
        dt,
        x_in,
        out_grad,
        decay_codes,
        decay_rate,
        skip_gain,
        scalars=(7, 8),
        far=(4, 5, 6),
    )
    grad_b, grad_c = kernel(
        total_kernel, "total", [((rows, STATE), F32)] * 2, totals, kept=False
    )
    return ssm_out, input_grad, grad_b, grad_c


def solution(mesh):
    placed = (
        P("seq", "head"),
        P(("seq", "head"), None),
        P(("seq", "head"), None),
        P("head", "seq"),
        P("head"),
        P("head"),
        P("seq", "head"),
    )
    return jax.shard_map(
        local,
        mesh=mesh,
        in_specs=placed,
        out_specs=(
            P("seq", "head"),
            P("seq", "head"),
            P(("seq", "head"), None),
            P(("seq", "head"), None),
        ),
        check_vma=False,
    )
```

```python
import jax
import jax.numpy as jnp
from jax import lax
from jax.experimental import pallas as pl
from jax.experimental.pallas import tpu as pltpu
from jax.sharding import PartitionSpec as P

HEAD_DIM = 64
STATE = 128
BLOCK = 256
BF = jnp.bfloat16
F32 = jnp.float32
HEAD_START = 8
SEQ_START = 21


def turned(count, start):
    start = start if start < count else 0
    return [(k + start) % count for k in range(count)]


def dg(a, b, ca, cb):
    return lax.dot_general(a, b, (((ca,), (cb,)), ((), ())), preferred_element_type=F32)


def pieces(v, count):
    out = []
    for _ in range(count):
        part = v.astype(BF)
        out.append(part)
        v = v - part.astype(F32)
    return out


def split_dot(v, b, ca, cb):
    hi, lo = pieces(v, 2)
    return dg(hi, b, ca, cb) + dg(lo, b, ca, cb)


def stack(rows, count):
    return jnp.concatenate([p.astype(F32) for p in pieces(rows, count)], axis=0).astype(BF)


def expand(stacked, heads):
    shape = (stacked.shape[0], heads * HEAD_DIM)
    row = lax.broadcasted_iota(jnp.int32, shape, 0) % heads
    col = lax.broadcasted_iota(jnp.int32, shape, 1) // HEAD_DIM
    pick = jnp.where(row == col, 1.0, 0.0).astype(BF)
    return dg(stacked, pick, 0, 0)


def decode(codes, rate_ref):
    heads, tokens = codes.shape
    head = lax.broadcasted_iota(jnp.int32, (heads, tokens), 0)
    rate = jnp.zeros((heads, tokens), F32)
    for h in range(heads):
        rate = jnp.where(head == h, rate_ref[h], rate)
    delta = 0.5 + (codes & 1023).astype(F32) / 1024.0
    log_decay = -rate * delta - 0.1 * (codes >> 10).astype(F32)
    return delta, log_decay


def running_sum(log_decay):
    tokens = log_decay.shape[1]
    i = lax.broadcasted_iota(jnp.int32, (tokens, tokens), 0)
    j = lax.broadcasted_iota(jnp.int32, (tokens, tokens), 1)
    upper = jnp.where(i <= j, 1.0, 0.0).astype(BF)
    return sum(dg(p, upper, 1, 0) for p in pieces(log_decay, 3)[::-1])


def both(bc_ref):
    groups, half = bc_ref.shape[0], bc_ref.shape[1] // 2
    order = turned(groups, HEAD_START)
    b, c = [
        jnp.concatenate([bc_ref[order.index(g), rows, :] for g in range(groups)], axis=0)
        for rows in (slice(0, half), slice(half, 2 * half))
    ]
    return b, c


def causal_mask():
    i = lax.broadcasted_iota(jnp.int32, (BLOCK, BLOCK), 0)
    j = lax.broadcasted_iota(jnp.int32, (BLOCK, BLOCK), 1)
    return i >= j


def weight_maker(log_decay, cumul):
    causal = causal_mask()
    lower = jnp.where(causal, 1.0, 0.0).astype(BF)
    cumul_t = sum(dg(lower, p, 1, 1) for p in pieces(log_decay, 3)[::-1])

    def weights(h):
        spread = cumul_t[:, h : h + 1] - cumul[h : h + 1, :]
        return jnp.exp(jnp.where(causal, spread, -1e30))

    return weights


def pair_cut(pair):
    return slice(pair * 2 * HEAD_DIM, (pair + 1) * 2 * HEAD_DIM)


def first_half():
    return lax.broadcasted_iota(jnp.int32, (BLOCK, 2 * HEAD_DIM), 1) < HEAD_DIM


def prepare_kernel(
    x_ref, dy_ref, codes_ref, rate_ref, td_ref, gd_ref, pr_ref, grow_ref, dt_ref, e_ref
):
    delta, log_decay = decode(codes_ref[...], rate_ref)
    cumul = running_sum(log_decay)
    heads = delta.shape[0]
    total = cumul[:, BLOCK - 1 :]
    growth = stack(jnp.exp(cumul), 3)
    tail = jnp.exp(total - cumul)
    driven = (x_ref[...].astype(F32) * expand(stack(delta, 2), heads)).astype(BF)
    td_ref[0], td_ref[1] = pieces(driven.astype(F32) * expand(stack(tail, 3), heads), 2)
    gd_ref[0], gd_ref[1] = pieces(dy_ref[...].astype(F32) * expand(growth, heads), 2)
    grow_ref[...] = growth
    dt_ref[...] = stack(delta * tail, 3)
    weights = weight_maker(log_decay, cumul)
    first = first_half()
    zero = jnp.zeros((BLOCK, 2 * HEAD_DIM), BF)
    paired = jnp.zeros((BLOCK, BLOCK), F32)
    for pair in range(heads // 2):
        u, g = driven[:, pair_cut(pair)], dy_ref[:, pair_cut(pair)]
        for side in range(2):
            own = first if side == 0 else jnp.logical_not(first)
            raw = dg(jnp.where(own, g, zero), u, 1, 1)
            paired = paired + (weights(2 * pair + side) * raw).astype(BF).astype(F32)
    pr_ref[0], pr_ref[1] = pieces(paired.T, 2)
    pr_ref[2], pr_ref[3] = pieces(paired, 2)
    hi, mid, low = [p.astype(F32) for p in pieces(jnp.exp(total), 3)]
    row = lax.broadcasted_iota(jnp.int32, (8, STATE), 0)
    for h in range(heads):
        e_ref[h] = jnp.where(
            row == 0, hi[h : h + 1, :], jnp.where(row == 1, mid[h : h + 1, :], low[h : h + 1, :])
        ).astype(BF)


def summary_kernel(bc_ref, td_ref, gd_ref, e_ref, send_ref):
    b, c = both(bc_ref)
    parts, heads = send_ref.shape[0], e_ref.shape[0]
    state = dg(td_ref[0], b, 0, 0) + dg(td_ref[1], b, 0, 0)
    adjoint = dg(gd_ref[0], c, 0, 0) + dg(gd_ref[1], c, 0, 0)
    send_ref[:, 0:16, :] = state.astype(BF).reshape(parts, 16, STATE)
    send_ref[:, 16:32, :] = adjoint.astype(BF).reshape(parts, 16, STATE)
    per = parts // heads
    for h in range(heads):
        for q in range(per):
            send_ref[h * per + q, 32:40, :] = e_ref[h]


def scan_kernel(got_ref, send_ref):
    count = got_ref.shape[0]
    order = turned(count, SEQ_START)
    slots = [order.index(k) for k in range(count)]
    decays = {}
    for k in slots:
        tile = got_ref[k, 32:40, :].astype(F32)
        decays[k] = tile[0:1] + tile[1:2] + tile[2:3]
    ahead = behind = jnp.zeros((16, STATE), F32)
    for k, m in zip(slots, slots[::-1]):
        send_ref[k, 0:16, :] = ahead.astype(BF)
        send_ref[m, 16:32, :] = behind.astype(BF)
        ahead = decays[k] * ahead + got_ref[k, 0:16, :].astype(F32)
        behind = decays[m] * behind + got_ref[m, 16:32, :].astype(F32)


def sums_kernel(bc_ref, in_ref, pr_ref, td_ref, gd_ref, sums_ref):
    b, c = both(bc_ref)
    width = td_ref.shape[2]
    groups, rows = sums_ref.shape[0], sums_ref.shape[1] // 2
    order = turned(groups, HEAD_START)
    for side, (parts, other) in enumerate(((td_ref, c), (gd_ref, b))):
        carry = in_ref[:, 16 - 16 * side : 32 - 16 * side, :].reshape(width, STATE)
        made = dg(pr_ref[2 * side], other, 1, 0) + dg(pr_ref[2 * side + 1], other, 1, 0)
        made = (made + dg(parts[0], carry, 1, 0) + dg(parts[1], carry, 1, 0)).astype(BF)
        for slot, g in enumerate(order):
            sums_ref[slot, side * rows : (side + 1) * rows, :] = made[g * rows : (g + 1) * rows]


def finish_kernel(
    bc_ref, in_ref, grow_ref, dt_ref, x_ref, dy_ref, codes_ref, rate_ref, gain_ref, out_ref, grad_ref
):
    b, c = both(bc_ref)
    delta, log_decay = decode(codes_ref[...], rate_ref)
    cumul = running_sum(log_decay)
    heads = delta.shape[0]
    width = heads * HEAD_DIM
    delta_x = expand(stack(delta, 2), heads)
    driven = (x_ref[...].astype(F32) * delta_x).astype(BF)
    state = in_ref[:, 0:16, :].reshape(width, STATE)
    adjoint = in_ref[:, 16:32, :].reshape(width, STATE)
    out_cross = expand(grow_ref[...], heads) * dg(c, state, 1, 1)
    grad_cross = expand(dt_ref[...], heads) * dg(b, adjoint, 1, 1)
    scores = dg(c, b, 1, 1)
    weights = weight_maker(log_decay, cumul)
    first = first_half()
    chan = lax.broadcasted_iota(jnp.int32, (1, 2 * HEAD_DIM), 1)
    for pair in range(heads // 2):
        cut = pair_cut(pair)
        u, g = driven[:, cut], dy_ref[:, cut]
        made = []
        for side in range(2):
            mixed = (weights(2 * pair + side) * scores).astype(BF)
            made.append((dg(mixed, u, 1, 0), dg(mixed, g, 0, 0)))
        gain = jnp.where(chan < HEAD_DIM, gain_ref[2 * pair], gain_ref[2 * pair + 1])
        out = jnp.where(first, made[0][0], made[1][0]) + out_cross[:, cut]
        grad = jnp.where(first, made[0][1], made[1][1]) * delta_x[:, cut] + grad_cross[:, cut]
        out_ref[:, cut] = (out + gain * x_ref[:, cut].astype(F32)).astype(BF)
        grad_ref[:, cut] = (grad + gain * g.astype(F32)).astype(BF)


def total_kernel(got_ref, b_ref, c_ref):
    acc = got_ref[0].astype(F32)
    for k in range(1, got_ref.shape[0]):
        acc = acc + got_ref[k].astype(F32)
    rows = b_ref.shape[0]
    b_ref[...] = acc[0:rows]
    c_ref[...] = acc[rows:]


def exchange(x, axis):
    count = lax.axis_size(axis)
    order = turned(count, HEAD_START if axis == "head" else SEQ_START)
    return lax.all_to_all(x, axis, 0, 0, tiled=True, axis_index_groups=[order])


def near(x):
    return pltpu.with_memory_space_constraint(x, pltpu.VMEM)


def kernel(body, name, outs, *args, scalars=(), far=(), kept=True):
    args = [x if i in scalars or i in far else near(x) for i, x in enumerate(args)]
    specs = [
        pl.BlockSpec(memory_space=pltpu.SMEM if i in scalars else pltpu.VMEM)
        for i in range(len(args))
    ]
    shapes = tuple(
        pltpu.VMEM(s, d) if kept else jax.ShapeDtypeStruct(s, d) for s, d in outs
    )
    got = pl.pallas_call(
        body,
        out_shape=shapes,
        in_specs=specs,
        out_specs=tuple(pl.BlockSpec(memory_space=pltpu.VMEM) for _ in outs),
        compiler_params=pltpu.CompilerParams(vmem_limit_bytes=16 << 20),
        name=name,
    )(*args)
    return got if len(outs) > 1 else got[0]


def local(x_in, b_in, c_in, decay_codes, decay_rate, skip_gain, out_grad):
    seqs, groups = lax.axis_size("seq"), lax.axis_size("head")
    rows = b_in.shape[0]
    heads, tokens = decay_codes.shape
    wide = x_in.shape
    spread = [jnp.broadcast_to(v[None], (groups, rows, STATE)) for v in (b_in, c_in)]
    bc = exchange(jnp.concatenate(spread, axis=1), "head")
    td, gd, paired, grow, dt, e = kernel(
        prepare_kernel,
        "prepare",
        [
            ((2,) + wide, BF),
            ((2,) + wide, BF),
            ((4, tokens, tokens), BF),
            ((3 * heads, tokens), BF),
            ((3 * heads, tokens), BF),
            ((heads, 8, STATE), BF),
        ],
        x_in,
        out_grad,
        decay_codes,
        decay_rate,
        scalars=(3,),
        far=(0, 1, 2),
    )
    send = kernel(summary_kernel, "summary", [((seqs, 40, STATE), BF)], bc, td, gd, e)
    got = exchange(send, "seq")
    back = kernel(scan_kernel, "scan", [((seqs, 32, STATE), BF)], got)
    carried = exchange(back, "seq")
    sums = kernel(
        sums_kernel, "sums", [((groups, 2 * rows, STATE), BF)], bc, carried, paired, td, gd
    )
    totals = exchange(sums, "head")
    ssm_out, input_grad = kernel(
        finish_kernel,
        "finish",
        [(wide, BF), (wide, BF)],
        bc,
        carried,
        grow,
        dt,
        x_in,
        out_grad,
        decay_codes,
        decay_rate,
        skip_gain,
        scalars=(7, 8),
        far=(4, 5, 6),
    )
    grad_b, grad_c = kernel(
        total_kernel, "total", [((rows, STATE), F32)] * 2, totals, kept=False
    )
    return ssm_out, input_grad, grad_b, grad_c


def solution(mesh):
    placed = (
        P("seq", "head"),
        P(("seq", "head"), None),
        P(("seq", "head"), None),
        P("head", "seq"),
        P("head"),
        P("head"),
        P("seq", "head"),
    )
    return jax.shard_map(
        local,
        mesh=mesh,
        in_specs=placed,
        out_specs=(
            P("seq", "head"),
            P("seq", "head"),
            P(("seq", "head"), None),
            P(("seq", "head"), None),
        ),
        check_vma=False,
    )
```
